128 devices in a mesh: sec: 2 (over y_lo), gx: 8 (over z, core), gy: 8 (over x, y_hi).
Axes of the slice: x: 4, y: 4 (y_hi: 2, y_lo: 2; y = y_hi * 2 + y_lo), z: 4, core: 2. Of those that a mesh axis runs over, the one named last changes fastest.
Arguments:
- atm_flux: bfloat16 [20480, 8, 128], P(('sec', 'gx', 'gy')), may hold values from -6 to 6
- remap_weights: bfloat16 [81920, 128, 128], P(('sec', 'gx', 'gy')), may hold values from -0.25 to 0.25
- remap_src: int32 [81920], P(('sec', 'gx', 'gy')), may hold values from 0 to 159
- remap_dst: int32 [81920], P(('sec', 'gx', 'gy')), may hold values from 0 to 127
- remap_owner: int32 [81920, 1], P(('sec', 'gx', 'gy')), may hold values from 0 to 127; in each aligned block of 640 rows (0 to 639, 640 to 1279, ...) at most 10 rows name the same one
- tracers: float32 [2, 16, 2048, 1024], P(None, None, ('sec', 'gx'), 'gy'), may hold values from -6 to 6
- currents: float32 [2, 16, 2048, 1024], P(None, None, ('sec', 'gx'), 'gy'), may hold values from -4 to 4
- land_sea: int32 [2048, 1024], P(('sec', 'gx'), 'gy'), may hold values 0 or 1
Outputs:
- tracers_out: float32 [2, 16, 2048, 1024], P(None, None, ('sec', 'gx'), 'gy')
- atmosphere_surface_temp: float32 [20480, 128], P(('sec', 'gx', 'gy'))
The draws below stay inside these ranges and needn't reach their ends.
Inputs may be any that keep to these rules, and one draw needn't show every extreme that they name: `remap_owner`: among the 640 nonzero blocks of each device, no ocean device is named more than 10 times; some ocean device is named exactly 10 times.
All inputs are finite; a program needn't handle non-finite values. No bound on the sum of `land_sea` on one device may be relied on, other than what follows from the above.
Results may differ from the reference program's by a relative error of at most 0.0031.
Values may be sent and summed in bfloat16 or wider, within the bound.
A program may use at most 128 MiB of HBM per device.

```python
import math
import jax
import jax.numpy as jnp
import numpy as np
from jax import lax

REMAP_CELLS = 128
NF = 8
NL = 16
FANOUT = 4
ATMOS_BLOCKS = 160
CX = 128
NNZ_DEV = 640
CAP = 10
A_BLOCKS = 20480
NNZ = 81920
OCEAN_ROW_COUNT = 2048
NY = 1024
N_SEC = 2
N_GX = 8
N_GY = 8
DEVICES = 128


def place_ends(result, key, smallest, largest):
    index_at = [jax.random.randint(jax.random.fold_in(key, axis), (), 0, length) for axis, length in enumerate(result.shape)]
    widest = result.shape.index(max(result.shape))
    next_to = index_at[:widest] + [(index_at[widest] + 1) % result.shape[widest]] + index_at[widest + 1:]
    return result.at[tuple(index_at)].set(smallest).at[tuple(next_to)].set(largest)


def shard_levels(stream_key, shape, split, low, high):
    loudness = 1.0
    for axis_at, shards_of in split:
        steps = jax.random.uniform(jax.random.fold_in(jax.random.fold_in(stream_key, 6), axis_at), (shards_of,), jnp.float32, low / len(split), high / len(split))
        loudness = loudness * jnp.repeat(jnp.exp(steps), shape[axis_at] // shards_of).reshape((-1,) + (1,) * (len(shape) - 1 - axis_at))
    return loudness


def shared_out(stream_key, own, number, rows, count, top, reach, slope):
    order = jax.random.permutation(stream_key, count)
    heavy_load, usual = shares(count, rows * top, reach, slope, True), shares(count, rows * top, reach, slope, False)
    places = jnp.arange(count)

    def named(sizes, offset_by):
        used = int((sizes > 0).sum())
        fixed = max(1, used // 4)
        shifted = fixed + (places - fixed + offset_by * (used - fixed)) % max(1, count - fixed)
        return jnp.zeros((count,), jnp.int32).at[order[jnp.where(places < fixed, places, shifted)]].set(jnp.asarray(sizes, jnp.int32))

    sizes = jnp.where(number % 4 == 0, named(heavy_load, number // 4), named(usual, number - number // 4 - 1))
    mixed = jax.random.permutation(jax.random.fold_in(own, 3), count)
    donor, receiver = mixed[0:count // 2 * 2:2], mixed[1:count // 2 * 2:2]
    margin = jnp.minimum(sizes[donor] - 1, reach - sizes[receiver]) // 2
    margin = jnp.where((donor == order[0]) | (receiver == order[0]) | (sizes[receiver] == 0), 0, jnp.maximum(margin, 0))
    shifted = jax.random.randint(jax.random.fold_in(own, 4), (count // 2,), 0, 1 << 20) % (margin + 1)
    sizes = sizes.at[donor].add(-shifted).at[receiver].add(shifted)
    members = jnp.searchsorted(jnp.cumsum(sizes), jnp.arange(rows * top), side="right").astype(jnp.int32)
    table = members.reshape(top, rows).T
    table = table[jax.random.permutation(jax.random.fold_in(own, 1), rows)]
    offset_by = jax.random.randint(jax.random.fold_in(own, 2), (rows, 1), 0, top)
    return jnp.take_along_axis(table, (jnp.arange(top)[None, :] + offset_by) % top, axis=1)


def shares(amount, total, reach, slope, full):
    weights = [(1 << 20) // math.isqrt(rank ** slope) + 1 for rank in range(1, amount + 1)]
    largest = reach if full else min(reach, max(-(-total // amount), total * weights[0] // sum(weights)))
    least = 1 if total - largest >= amount - 1 else 0
    given, surplus = [largest] + [least] * (amount - 1), total - largest - least * (amount - 1)
    while surplus > 0:
        candidates = [i for i in range(1, amount) if given[i] < largest] or [i for i in range(1, amount) if given[i] < reach]
        mass, remaining = sum([weights[i] for i in candidates]), surplus
        for i in candidates:
            more = min(reach - given[i], max(1, remaining * weights[i] // mass), surplus)
            given[i] = given[i] + more
            surplus = surplus - more
    return np.array(given)


def noise(stream_key, shape, width, reach, split=(), kind=jnp.bfloat16):
    gain = shard_levels(stream_key, shape, split, -0.22, 0.18) if split else 1.0
    values = jax.random.normal(stream_key, shape, jnp.float32) * width * gain
    return jnp.minimum(jnp.maximum(values, -reach), reach).astype(kind)


def setup_inputs(seed: int = 0) -> dict:
    arg_keys = jax.random.split(jax.random.key(seed), 9)
    atm_flux = noise(arg_keys[0], (A_BLOCKS, NF, REMAP_CELLS), 1.0, 6.0, ((0, 128),))
    remap_weights = noise(arg_keys[1], (NNZ, REMAP_CELLS, REMAP_CELLS), (REMAP_CELLS * FANOUT * ATMOS_BLOCKS // CX) ** -0.5, 0.25, ((0, 128),))
    remap_src = place_ends(jax.random.randint(arg_keys[2], (NNZ,), 0, ATMOS_BLOCKS), jax.random.fold_in(arg_keys[2], 1), 0, ATMOS_BLOCKS - 1).astype(jnp.int32)
    remap_dst = place_ends(jax.random.randint(arg_keys[3], (NNZ,), 0, CX), jax.random.fold_in(arg_keys[3], 1), 0, CX - 1).astype(jnp.int32)
    remap_owner_keys = jax.random.split(jax.random.fold_in(arg_keys[4], 1), NNZ // NNZ_DEV)
    remap_owner_turns = jax.random.permutation(jax.random.fold_in(arg_keys[4], 3), NNZ // NNZ_DEV)
    remap_owner = jax.vmap(lambda own, number: shared_out(jax.random.fold_in(arg_keys[4], 2), own, number, NNZ_DEV, DEVICES, 1, CAP, 1))(remap_owner_keys, remap_owner_turns).reshape((NNZ, 1))
    tracers = noise(arg_keys[5], (2, NL, OCEAN_ROW_COUNT, NY), 1.0, 6.0, ((2, 16), (3, 8)), jnp.float32)
    currents = noise(arg_keys[6], (2, NL, OCEAN_ROW_COUNT, NY), 0.3, 4.0, ((2, 16), (3, 8)), jnp.float32)
    land_sea = place_ends((jax.random.randint(arg_keys[7], (OCEAN_ROW_COUNT, NY), 0, 10) < 7).astype(jnp.int32), jax.random.fold_in(arg_keys[7], 1), 0, 1)
    return {"atm_flux": atm_flux, "remap_weights": remap_weights, "remap_src": remap_src, "remap_dst": remap_dst, "remap_owner": remap_owner, "tracers": tracers, "currents": currents, "land_sea": land_sea}


KH = 0.1
KV = 0.1


def substep(tracer_field, velocity, wetness, heat, salt, shortwave):
    levels = tracer_field.shape[1]
    centre = tracer_field[..., 1:-1, 1:-1]
    east = tracer_field[..., 1:-1, 2:]
    west = tracer_field[..., 1:-1, :-2]
    north = tracer_field[..., 2:, 1:-1]
    south = tracer_field[..., :-2, 1:-1]
    wet_centre = wetness[1:-1, 1:-1]
    open_east = wet_centre * wetness[1:-1, 2:]
    open_west = wet_centre * wetness[1:-1, :-2]
    open_north = wet_centre * wetness[2:, 1:-1]
    open_south = wet_centre * wetness[:-2, 1:-1]
    u_along = velocity[0]
    v_along = velocity[1]
    flow_east = 0.5 * (u_along[:, 1:-1, 1:-1] + u_along[:, 1:-1, 2:]) * open_east
    flow_west = 0.5 * (u_along[:, 1:-1, :-2] + u_along[:, 1:-1, 1:-1]) * open_west
    flow_north = 0.5 * (v_along[:, 1:-1, 1:-1] + v_along[:, 2:, 1:-1]) * open_north
    flow_south = 0.5 * (v_along[:, :-2, 1:-1] + v_along[:, 1:-1, 1:-1]) * open_south
    advect = -(flow_east * 0.5 * (centre + east) - flow_west * 0.5 * (west + centre)
               + flow_north * 0.5 * (centre + north) - flow_south * 0.5 * (south + centre))
    spread = KH * (open_east * (east - centre) + open_west * (west - centre)
                   + open_north * (north - centre) + open_south * (south - centre))
    mixing = KV * (centre[:, 1:] - centre[:, :-1])
    blank = jnp.zeros_like(centre[:, :1])
    vertical = jnp.concatenate([mixing, blank], axis=1) - jnp.concatenate([blank, mixing], axis=1)
    depth = jnp.arange(levels, dtype=jnp.float32)
    profile = jnp.exp(-depth / 4.0) * (1.0 - jnp.exp(jnp.float32(-0.25)))
    surface = (depth == 0.0).astype(jnp.float32)
    warm = 0.3 * profile[:, None, None] * shortwave[None] + surface[:, None, None] * heat[None]
    fresh = surface[:, None, None] * salt[None] + jnp.zeros_like(warm)
    forcing = jnp.stack([warm, fresh])
    return centre + wet_centre * (advect + spread + vertical + forcing)


def forcing_fields(ocean_flux, currents, levels):
    surface = (jnp.arange(levels) == 0).astype(jnp.float32)[:, None, None]
    u_eff = currents[0] + 0.1 * surface * ocean_flux[6][None]
    v_eff = currents[1] + 0.1 * surface * ocean_flux[7][None]
    heat = 0.2 * (ocean_flux[1] + ocean_flux[2] + ocean_flux[3]) - 0.15 * ocean_flux[5]
    salt = 0.2 * ocean_flux[4] - 0.1 * ocean_flux[5]
    return u_eff, v_eff, heat, salt, ocean_flux[0]


def reference(atm_flux, remap_weights, remap_src, remap_dst, remap_owner, tracers, currents, land_sea):
    device_list = N_SEC * N_GX * N_GY
    total = remap_src.shape[0]
    device_share = total // device_list
    device_of = (jnp.arange(total, dtype=jnp.int32) // device_share).astype(jnp.int32)
    worldwide_source = (device_of * ATMOS_BLOCKS + remap_src).astype(jnp.int32)
    owners = remap_owner[:, 0]
    ocean_row = ((owners // N_GY) * CX + remap_dst).astype(jnp.int32)
    marine_block = (ocean_row * N_GY + owners % N_GY).astype(jnp.int32)
    weight_groups = remap_weights.reshape(device_list, device_share, REMAP_CELLS, REMAP_CELLS)
    source_groups = worldwide_source.reshape(device_list, device_share)

    def forward(pair):
        weights, sources = pair
        rows = jnp.take(atm_flux, sources, axis=0).astype(jnp.float32)
        return jnp.einsum("kij,kfj->kfi", weights.astype(jnp.float32), rows).astype(jnp.bfloat16)

    partial_flux = lax.map(forward, (weight_groups, source_groups)).reshape(total, NF, REMAP_CELLS)
    blocks = jnp.zeros((OCEAN_ROW_COUNT * N_GY, NF, REMAP_CELLS), jnp.float32).at[marine_block].add(partial_flux.astype(jnp.float32))
    ocean_flux = blocks.reshape(OCEAN_ROW_COUNT, N_GY, NF, REMAP_CELLS).transpose(2, 0, 1, 3).reshape(NF, OCEAN_ROW_COUNT, N_GY * REMAP_CELLS)
    u_eff, v_eff, heat, salt, shortwave = forcing_fields(ocean_flux, currents, NL)
    wetness = jnp.pad(land_sea.astype(jnp.float32), 1)
    velocity = jnp.pad(jnp.stack([u_eff, v_eff]), ((0, 0), (0, 0), (1, 1), (1, 1)))
    tracer_field = tracers
    for repeat in range(2):
        padded = jnp.pad(tracer_field, ((0, 0), (0, 0), (1, 1), (1, 1)))
        tracer_field = substep(padded, velocity, wetness, heat, salt, shortwave)
    surface_temp_blocks = tracer_field[0, 0].astype(jnp.bfloat16).reshape(OCEAN_ROW_COUNT * N_GY, REMAP_CELLS)
    selected_cells = jnp.take(surface_temp_blocks, marine_block, axis=0).reshape(device_list, device_share, REMAP_CELLS)

    def backward(pair):
        weights, values = pair
        return jnp.einsum("kij,ki->kj", weights.astype(jnp.float32), values.astype(jnp.float32))

    returning_terms = lax.map(backward, (weight_groups, selected_cells)).reshape(total, REMAP_CELLS)
    atmosphere_surface_temp = jnp.zeros((device_list * ATMOS_BLOCKS, REMAP_CELLS), jnp.float32).at[worldwide_source].add(returning_terms)
    return tracer_field, atmosphere_surface_temp
```

```python
import functools

import jax
import jax.numpy as jnp
from jax import lax
from jax.experimental import pallas as pl
from jax.experimental.pallas import tpu as pltpu
from jax.sharding import PartitionSpec as P

KH = 0.1
KV = 0.1
CAP = 10
SLOTS = 16
KEPT = 5
LANES = 128
DEVICES = 128
LOGICAL = pl.DeviceIdType.LOGICAL
BF16 = jnp.bfloat16
F32 = jnp.float32


def extended_2(block, sides, width):
    for axis, dim in sides:
        count = lax.axis_size(axis)
        forward = [(i, i + 1) for i in range(count - 1)]
        backward = [(target, source) for source, target in forward]
        low = lax.ppermute(
            lax.slice_in_dim(block, block.shape[dim] - width, None, axis=dim), axis, forward
        )
        high = lax.ppermute(lax.slice_in_dim(block, 0, width, axis=dim), axis, backward)
        block = jnp.concatenate([low, block, high], axis=dim)
    return block


def substep(tracer_field, velocity, wetness, heat, salt, shortwave):
    levels = tracer_field.shape[1]
    centre = tracer_field[..., 1:-1, 1:-1]
    east = tracer_field[..., 1:-1, 2:]
    west = tracer_field[..., 1:-1, :-2]
    north = tracer_field[..., 2:, 1:-1]
    south = tracer_field[..., :-2, 1:-1]
    wet_centre = wetness[1:-1, 1:-1]
    open_east = wet_centre * wetness[1:-1, 2:]
    open_west = wet_centre * wetness[1:-1, :-2]
    open_north = wet_centre * wetness[2:, 1:-1]
    open_south = wet_centre * wetness[:-2, 1:-1]
    u_along = velocity[0]
    v_along = velocity[1]
    flow_east = 0.5 * (u_along[:, 1:-1, 1:-1] + u_along[:, 1:-1, 2:]) * open_east
    flow_west = 0.5 * (u_along[:, 1:-1, :-2] + u_along[:, 1:-1, 1:-1]) * open_west
    flow_north = 0.5 * (v_along[:, 1:-1, 1:-1] + v_along[:, 2:, 1:-1]) * open_north
    flow_south = 0.5 * (v_along[:, :-2, 1:-1] + v_along[:, 1:-1, 1:-1]) * open_south
    advect = -(
        flow_east * 0.5 * (centre + east)
        - flow_west * 0.5 * (west + centre)
        + flow_north * 0.5 * (centre + north)
        - flow_south * 0.5 * (south + centre)
    )
    spread = KH * (
        open_east * (east - centre)
        + open_west * (west - centre)
        + open_north * (north - centre)
        + open_south * (south - centre)
    )
    mixing = KV * (centre[:, 1:] - centre[:, :-1])
    vertical = jnp.pad(mixing, ((0, 0), (0, 1), (0, 0), (0, 0))) - jnp.pad(
        mixing, ((0, 0), (1, 0), (0, 0), (0, 0))
    )
    depth = jnp.arange(levels, dtype=jnp.float32)
    profile = jnp.exp(-depth / 4.0) * (1.0 - jnp.exp(jnp.float32(-0.25)))
    surface = (depth == 0.0).astype(jnp.float32)
    warm = 0.3 * profile[:, None, None] * shortwave[None] + surface[:, None, None] * heat[None]
    fresh = surface[:, None, None] * salt[None]
    is_temp = (jnp.arange(2) == 0)[:, None, None, None]
    forcing = jnp.where(is_temp, warm[None], fresh[None])
    return centre + wet_centre * (advect + spread + vertical + forcing)


def my_index():
    return lax.axis_index("sec") * 64 + lax.axis_index("gx") * 8 + lax.axis_index("gy")


def partner(t):
    sec, gx, gy = lax.axis_index("sec"), lax.axis_index("gx"), lax.axis_index("gy")
    core = (gx % 2 + t) % 2
    x = (gy // 2 + t // 2) % 4
    y = ((gy % 2) * 2 + sec + t // 8) % 4
    z = (gx // 2 + t // 32) % 4
    return (y % 2) * 64 + (z * 2 + core) * 8 + x * 2 + y // 2


def greet():
    barrier = pltpu.get_barrier_semaphore()

    def signal(t, carry):
        pl.semaphore_signal(barrier, inc=1, device_id=partner(t), device_id_type=LOGICAL)
        return carry

    lax.fori_loop(1, DEVICES, signal, 0)
    return barrier


def wait_others(ref, sem, rows):
    if len(ref.shape) == 4:
        view = ref.at[pl.ds(0, DEVICES - 1), :, pl.ds(0, rows)]
    else:
        view = ref.at[pl.ds(0, DEVICES - 1), pl.ds(0, rows)]
    pltpu.make_async_copy(view, view, sem).wait()


def weight_copy(w_hbm, w_ref, w_sem, chunk, size):
    part = pl.ds(chunk * size, size)
    return pltpu.make_async_copy(w_hbm.at[part], w_ref.at[part], w_sem.at[chunk])


CHUNK = 32


def forward_kernel(
    src_ref, kidx_ref, atm_ref, row_ref, w_hbm,
    rflux_ref, rrow_ref,
    w_ref, part_ref, tmp_ref, send_ref, srow_ref,
    w_sem, sends, recvs, rsends, rrecvs, lsem,
):
    me = my_index()
    nonzeros = w_ref.shape[0]
    chunks = nonzeros // CHUNK

    def start(c, carry):
        weight_copy(w_hbm, w_ref, w_sem, c, CHUNK).start()
        return carry

    lax.fori_loop(0, chunks, start, 0)
    rflux_ref[...] = jnp.zeros_like(rflux_ref)
    barrier = greet()
    srow_ref[:, 0:1, :] = row_ref[...].reshape(DEVICES, 1, LANES)
    part_ref[nonzeros] = jnp.zeros((8, LANES), F32)
    tmp_ref[...] = jnp.zeros_like(tmp_ref)
    sub = lax.broadcasted_iota(jnp.int32, (8, LANES), 0)
    paired = (sub == 1) | (sub == 2)

    def chunk_step(c, carry):
        weight_copy(w_hbm, w_ref, w_sem, c, CHUNK).wait()

        def group(g, inner):
            base = c * CHUNK + g * 16
            for i in range(16):
                k = base + i
                p = lax.dot_general(
                    atm_ref[src_ref[k]], w_ref[k], (((1,), (1,)), ((), ())),
                    preferred_element_type=F32,
                )
                part_ref[k] = p + jnp.where(paired, pltpu.roll(p, 4, 0), 0.0)
            return inner

        return lax.fori_loop(0, CHUNK // 16, group, carry)

    lax.fori_loop(0, chunks, chunk_step, 0)
    pl.semaphore_wait(barrier, DEVICES - 1)

    def send_rows(t, carry):
        p = partner(t)
        pltpu.make_async_remote_copy(
            srow_ref.at[p, pl.ds(0, 1)], rrow_ref.at[me, pl.ds(0, 1)], rsends, rrecvs,
            device_id=p, device_id_type=LOGICAL,
        ).start()
        return carry

    lax.fori_loop(1, DEVICES, send_rows, 0)

    def send_one(p):
        pltpu.make_async_remote_copy(
            send_ref.at[p, :, pl.ds(0, CAP)], rflux_ref.at[me, :, pl.ds(0, CAP)], sends, recvs,
            device_id=p, device_id_type=LOGICAL,
        ).start()

    def pack(i, last):
        p = partner(DEVICES - 1 - i)
        for s in range(CAP):
            tmp_ref[s * 8 : s * 8 + 8, :] = part_ref[kidx_ref[p * CAP + s]]
        for f in range(KEPT):
            send_ref[p, f] = tmp_ref[pl.ds(f, SLOTS, stride=8), :].astype(BF16)

        @pl.when(i > 0)
        def _():
            send_one(last)

        return p

    lax.fori_loop(0, DEVICES, pack, me)
    own = pltpu.make_async_copy(send_ref.at[me], rflux_ref.at[me], lsem.at[0])
    own.start()
    own_row = pltpu.make_async_copy(srow_ref.at[me], rrow_ref.at[me], lsem.at[1])
    own_row.start()
    own.wait()
    own_row.wait()
    wait_others(srow_ref, rsends, 1)
    wait_others(rrow_ref, rrecvs, 1)
    wait_others(send_ref, sends, CAP)
    wait_others(rflux_ref, recvs, CAP)


def backward_kernel(
    slot_ref, src_row_ref, send_ref, w_hbm,
    out_ref,
    w_ref, ret_ref, ret32_ref, terms_ref,
    w_sem, sends, recvs, lsem,
):
    me = my_index()
    nonzeros = w_ref.shape[0]
    chunks = nonzeros // CHUNK

    def start(c, carry):
        weight_copy(w_hbm, w_ref, w_sem, c, CHUNK).start()
        return carry

    lax.fori_loop(0, chunks, start, 0)
    barrier = greet()
    pl.semaphore_wait(barrier, DEVICES - 1)

    def send_one(t, carry):
        p = partner(DEVICES - t)
        pltpu.make_async_remote_copy(
            send_ref.at[p, pl.ds(0, CAP)], ret_ref.at[me, pl.ds(0, CAP)], sends, recvs,
            device_id=p, device_id_type=LOGICAL,
        ).start()
        return carry

    lax.fori_loop(1, DEVICES, send_one, 0)
    own = pltpu.make_async_copy(
        send_ref.at[me, pl.ds(0, CAP)], ret_ref.at[me, pl.ds(0, CAP)], lsem
    )
    own.start()
    own.wait()
    wait_others(send_ref, sends, CAP)
    wait_others(ret_ref, recvs, CAP)
    ret32_ref[...] = ret_ref[...].astype(F32).reshape(ret32_ref.shape)
    sub = lax.broadcasted_iota(jnp.int32, (8, LANES), 0)

    def chunk_step(c, carry):
        weight_copy(w_hbm, w_ref, w_sem, c, CHUNK).wait()

        def group(g, inner):
            base = c * CHUNK + g * 8
            rows = jnp.concatenate(
                [ret32_ref[pl.ds(slot_ref[base + i], 1), :] for i in range(8)], axis=0
            )
            left = jnp.concatenate(
                [jnp.where(sub == i, rows, 0.0).astype(BF16) for i in range(8)], axis=1
            )
            right = w_ref[pl.ds(base, 8)].reshape(8 * LANES, LANES)
            terms_ref[pl.ds(pl.multiple_of(base, 8), 8), :] = jnp.dot(
                left, right, preferred_element_type=F32
            )
            return inner

        return lax.fori_loop(0, CHUNK // 8, group, carry, unroll=True)

    lax.fori_loop(0, chunks, chunk_step, 0)
    blocks = out_ref.shape[0]
    hot = (
        lax.broadcasted_iota(jnp.int32, (blocks, nonzeros), 0) == src_row_ref[...]
    ).astype(F32).astype(BF16)
    terms = terms_ref[...]
    high = terms.astype(BF16)
    rest = terms - high.astype(F32)
    mid = rest.astype(BF16)
    low = (rest - mid.astype(F32)).astype(BF16)
    out_ref[...] = (
        jnp.dot(hot, high, preferred_element_type=F32)
        + jnp.dot(hot, mid, preferred_element_type=F32)
        + jnp.dot(hot, low, preferred_element_type=F32)
    )


VMEM = pl.BlockSpec(memory_space=pltpu.VMEM)
SMEM = pl.BlockSpec(memory_space=pltpu.SMEM)
ANY = pl.BlockSpec(memory_space=pl.ANY)
LIMIT = 64000 * 1024


def on_device(
    atm_flux, remap_weights, remap_src, remap_dst, remap_owner, tracers, currents, land_sea
):
    nonzeros = remap_weights.shape[0]
    marine_rows = tracers.shape[2]
    levels = tracers.shape[1]
    width = remap_weights.shape[1]
    atm_blocks = atm_flux.shape[0]
    chunks = nonzeros // CHUNK

    owners = remap_owner[:, 0]
    hot = (owners[:, None] == jnp.arange(DEVICES, dtype=jnp.int32)[None, :]).astype(BF16)
    order = jnp.arange(nonzeros, dtype=jnp.int32)
    before = (order[:, None] > order[None, :]).astype(BF16)
    earlier = jnp.dot(before, hot, preferred_element_type=F32)
    position = jnp.sum(earlier * hot.astype(F32), axis=1).astype(jnp.int32)
    slot = owners * CAP + position
    taken = jnp.arange(DEVICES * CAP, dtype=jnp.int32)[:, None] == slot[None, :]
    kidx = jnp.sum(jnp.where(taken, order[None, :] - nonzeros, 0), axis=1) + nonzeros
    slot_rows = jnp.sum(jnp.where(taken, remap_dst[None, :] - 200, 0), axis=1) + 200
    row_table = jnp.pad(
        slot_rows.reshape(DEVICES, CAP).astype(F32), ((0, 0), (0, LANES - CAP)),
        constant_values=200.0,
    )
    f32 = atm_flux.astype(F32)
    warm = f32[:, 1] + f32[:, 2] + f32[:, 3] - 0.75 * f32[:, 5]
    fresh = f32[:, 4] - 0.5 * f32[:, 5]
    warm_high = lax.reduce_precision(warm, 8, 7)
    fresh_high = lax.reduce_precision(fresh, 8, 7)
    mixed = jnp.stack(
        [
            f32[:, 0], warm_high, fresh_high, f32[:, 6], f32[:, 7],
            warm - warm_high, fresh - fresh_high, jnp.zeros_like(warm),
        ],
        axis=1,
    ).astype(BF16)

    got, got_rows = pl.pallas_call(
        forward_kernel,
        name="forward",
        out_shape=[
            jax.ShapeDtypeStruct((DEVICES, KEPT, SLOTS, width), BF16),
            jax.ShapeDtypeStruct((DEVICES, 8, LANES), F32),
        ],
        in_specs=[SMEM, SMEM, VMEM, VMEM, ANY],
        out_specs=[VMEM, VMEM],
        scratch_shapes=[
            pltpu.VMEM(remap_weights.shape, BF16),
            pltpu.VMEM((nonzeros + 1, 8, LANES), F32),
            pltpu.VMEM((SLOTS * 8, LANES), F32),
            pltpu.VMEM((DEVICES, KEPT, SLOTS, width), BF16),
            pltpu.VMEM((DEVICES, 8, LANES), F32),
            pltpu.SemaphoreType.DMA((chunks,)),
            pltpu.SemaphoreType.DMA,
            pltpu.SemaphoreType.DMA,
            pltpu.SemaphoreType.DMA,
            pltpu.SemaphoreType.DMA,
            pltpu.SemaphoreType.DMA((2,)),
        ],
        compiler_params=pltpu.CompilerParams(
            collective_id=0, has_side_effects=True, vmem_limit_bytes=LIMIT
        ),
    )(remap_src, kidx, mixed, row_table, remap_weights)

    received = got_rows[:, 0, :SLOTS].reshape(DEVICES * SLOTS)
    row_hot = (
        received[:, None] == jnp.arange(marine_rows, dtype=jnp.int32)[None, :].astype(F32)
    ).astype(BF16)
    shortwave, heat, salt, u_flux, v_flux = [
        lax.dot_general(
            row_hot, got[:, i].reshape(DEVICES * SLOTS, width), (((0,), (0,)), ((), ())),
            preferred_element_type=F32,
        )
        for i in range(KEPT)
    ]
    surface = (jnp.arange(levels) == 0).astype(F32)[:, None, None]
    u_eff = currents[0] + 0.1 * surface * u_flux[None]
    v_eff = currents[1] + 0.1 * surface * v_flux[None]
    wetness = land_sea.astype(F32)
    tracer_field = tracers
    statics = jnp.concatenate([u_eff, v_eff, wetness[None]], axis=0)
    statics = extended_2(statics, ((("sec", "gx"), 1), ("gy", 2)), 1)
    velocity = statics[: 2 * levels].reshape(2, levels, statics.shape[1], statics.shape[2])
    wet_ext = statics[2 * levels]
    for repeat in range(2):
        extended = extended_2(tracer_field, ((("sec", "gx"), 2), ("gy", 3)), 1)
        tracer_field = substep(extended, velocity, wet_ext, 0.2 * heat, 0.2 * salt, shortwave)
    surface_temp = tracer_field[0, 0].astype(BF16)
    returning = jnp.dot(row_hot, surface_temp, preferred_element_type=F32).astype(BF16)

    temp = pl.pallas_call(
        backward_kernel,
        name="backward",
        out_shape=jax.ShapeDtypeStruct((atm_blocks, width), F32),
        in_specs=[SMEM, VMEM, VMEM, ANY],
        out_specs=VMEM,
        scratch_shapes=[
            pltpu.VMEM(remap_weights.shape, BF16),
            pltpu.VMEM((DEVICES, SLOTS, width), BF16),
            pltpu.VMEM((DEVICES * SLOTS, width), F32),
            pltpu.VMEM((nonzeros, width), F32),
            pltpu.SemaphoreType.DMA((chunks,)),
            pltpu.SemaphoreType.DMA,
            pltpu.SemaphoreType.DMA,
            pltpu.SemaphoreType.DMA,
        ],
        compiler_params=pltpu.CompilerParams(
            collective_id=1, has_side_effects=True, vmem_limit_bytes=LIMIT
        ),
    )(
        owners * SLOTS + position, remap_src[None, :],
        returning.reshape(DEVICES, SLOTS, width), remap_weights,
    )
    return (tracer_field, temp)


def solution(mesh):
    return jax.shard_map(
        on_device,
        mesh=mesh,
        in_specs=(
            P(("sec", "gx", "gy"), None, None),
            P(("sec", "gx", "gy"), None, None),
            P(("sec", "gx", "gy")),
            P(("sec", "gx", "gy")),
            P(("sec", "gx", "gy"), None),
            P(None, None, ("sec", "gx"), "gy"),
            P(None, None, ("sec", "gx"), "gy"),
            P(("sec", "gx"), "gy"),
        ),
        out_specs=(P(None, None, ("sec", "gx"), "gy"), P(("sec", "gx", "gy"), None)),
        check_vma=False,
    )
```

```python
import math

import jax
import jax.numpy as jnp
from jax import lax
from jax.experimental import pallas as pl
from jax.experimental.pallas import tpu as pltpu
from jax.sharding import PartitionSpec as P

KH = 0.1
KV = 0.1
CAP = 10
SLOTS = 16
KEPT = (0, 1, 4, 6, 7)
LANES = 128
DEVICES = 128
CHUNK = 32
STRIP = 32
DECAY = math.exp(-0.25)
LOGICAL = pl.DeviceIdType.LOGICAL
MESH = pl.DeviceIdType.MESH
BF16 = jnp.bfloat16
F32 = jnp.float32
I32 = jnp.int32


class Torus:
    def __init__(self):
        sec, gx, gy = lax.axis_index("sec"), lax.axis_index("gx"), lax.axis_index("gy")
        self.band, self.gy = sec * 8 + gx, gy
        self.me = self.band * 8 + gy
        up, down = (self.band + 1) % 16, (self.band + 15) % 16
        self.north = (up // 8, up % 8, gy)
        self.south = (down // 8, down % 8, gy)
        self.east = (sec, gx, (gy + 1) % 8)
        self.west = (sec, gx, (gy + 7) % 8)
        self.y, self.z = (gy % 2) * 2 + sec, gx // 2
        self.xs = [((gy // 2 + d) % 4) * 2 for d in range(4)]
        self.cores = [((gx + d) % 2) * 8 for d in range(2)]

    def group(self, o):
        y = (self.y + 3 - o % 4) % 4
        z = (self.z + 3 - o // 4) % 4
        base = (y % 2) * 64 + y // 2 + z * 16
        return [base + self.xs[d] + self.cores[c] for d in (2, 1, 3, 0) for c in (1, 0)]

    def send_group(self, o, act):
        partners = self.group(o)
        for p in partners[:-1]:
            act(p)

        @pl.when(o < 15)
        def _():
            act(partners[-1])

    def each(self, act):
        def body(o, carry):
            self.send_group(o, act)
            return carry

        lax.fori_loop(0, 16, body, 0)


def wait_others(ref, sem, rows):
    first = pl.ds(0, DEVICES - 1)
    view = ref.at[first, :, pl.ds(0, rows)] if len(ref.shape) == 4 else ref.at[first, pl.ds(0, rows)]
    pltpu.make_async_copy(view, view, sem).wait()


def coupled_kernel(
    src_ref, kidx_ref, slot_ref, row_ref, srcrow_ref, atm_ref, land_ref, w_hbm, q_hbm, uv_hbm,
    out_hbm, temp_ref,
    w_ref, part_ref, tmp_ref, send_ref, got_ref, srow_ref, rrow_ref, hot_ref, hott_ref,
    flux_ref, sret_ref, ret_ref, ret32_ref, terms_ref, srchot_ref,
    q_ref, uv_ref, q1_ref, q2_ref, coef_ref, open_ref, wet_ref,
    pe_ref, pw_ref, he_ref, hw_ref, pn_ref, ps_ref, hn_ref, hs_ref,
    heu_ref, hwu_ref, hnv_ref, hsv_ref,
    he1_ref, hw1_ref, hn1_ref, hs1_ref,
    pe2_ref, pw2_ref, he2_ref, hw2_ref, pn2_ref, ps2_ref, hn2_ref, hs2_ref,
    w_sem, in_sem, a2a_send, a2a_recv, side_send, side_recv, own_sem, out_sem,
):
    here = Torus()
    nonzeros = w_ref.shape[0]
    chunks = nonzeros // CHUNK
    levels = q_ref.shape[1]
    inner = pl.ds(8, LANES)

    def weight_copy(c):
        part = pl.ds(c * CHUNK, CHUNK)
        return pltpu.make_async_copy(w_hbm.at[part], w_ref.at[part], w_sem.at[c])

    def start_weights(c, carry):
        weight_copy(c).start()
        return carry

    lax.fori_loop(0, chunks, start_weights, 0)
    q_copy = pltpu.make_async_copy(q_hbm, q_ref.at[:, :, inner], in_sem.at[0])
    uv_copy = pltpu.make_async_copy(uv_hbm, uv_ref.at[:, :, inner], in_sem.at[1])
    q_copy.start()
    uv_copy.start()

    got_ref[...] = jnp.zeros_like(got_ref)
    barrier = pltpu.get_barrier_semaphore()
    here.each(
        lambda p: pl.semaphore_signal(barrier, inc=1, device_id=p, device_id_type=LOGICAL)
    )
    srow_ref[:, 0:1, :] = row_ref[...].reshape(DEVICES, 1, LANES)
    part_ref[nonzeros] = jnp.zeros((8, LANES), F32)
    tmp_ref[...] = jnp.zeros_like(tmp_ref)
    pn_ref[...] = jnp.zeros_like(pn_ref)
    ps_ref[...] = jnp.zeros_like(ps_ref)
    pe_ref[...] = jnp.zeros_like(pe_ref)
    pw_ref[...] = jnp.zeros_like(pw_ref)
    pe2_ref[...] = jnp.zeros_like(pe2_ref)
    pn2_ref[...] = jnp.zeros_like(pn2_ref)
    ps2_ref[...] = jnp.zeros_like(ps2_ref)
    pw2_ref[...] = jnp.zeros_like(pw2_ref)

    sub = lax.broadcasted_iota(I32, (8, LANES), 0)
    keep = jnp.where((sub == 2) | (sub == 3) | (sub == 5), 0.0, 1.0)
    one_up = jnp.where(sub == 1, 1.0, jnp.where(sub == 4, -0.5, 0.0))
    two_up = jnp.where(sub == 1, 1.0, 0.0)
    four_up = jnp.where(sub == 1, -0.75, 0.0)
    blank = jnp.zeros((8, LANES), BF16)

    def combine(p):
        p = p.astype(BF16).astype(F32)
        return (
            p * keep
            + pltpu.roll(p, 7, 0) * one_up
            + pltpu.roll(p, 6, 0) * two_up
            + pltpu.roll(p, 4, 0) * four_up
        )

    def forward(c, carry):
        weight_copy(c).wait()
        for i in range(0, CHUNK, 2):
            k = c * CHUNK + i
            left = jnp.concatenate(
                [
                    jnp.concatenate([atm_ref[src_ref[k]], blank], axis=1),
                    jnp.concatenate([blank, atm_ref[src_ref[k + 1]]], axis=1),
                ],
                axis=0,
            )
            right = jnp.concatenate([w_ref[k], w_ref[k + 1]], axis=1)
            p = lax.dot_general(
                left, right, (((1,), (1,)), ((), ())), preferred_element_type=F32
            )
            part_ref[k] = combine(p[:8])
            part_ref[k + 1] = combine(p[8:])
        return carry

    lax.fori_loop(0, chunks, forward, 0)
    pl.semaphore_wait(barrier, DEVICES - 1)

    def all_to_all(index, src, dst, cut):
        def act(p):
            pltpu.make_async_remote_copy(
                cut(src, p), cut(dst, here.me), a2a_send.at[index], a2a_recv.at[index],
                device_id=p, device_id_type=LOGICAL,
            ).start()

        return act

    here.each(all_to_all(0, srow_ref, rrow_ref, lambda ref, i: ref.at[i, pl.ds(0, 1)]))
    send_flux = all_to_all(1, send_ref, got_ref, lambda ref, i: ref.at[i, :, pl.ds(0, CAP)])

    def pack(o, carry):
        partners = here.group(o)
        for i, p in enumerate(partners):
            for s in range(CAP):
                tmp_ref[i, s * 8 : s * 8 + 8, :] = part_ref[kidx_ref[p * CAP + s]]
        for i, p in enumerate(partners):
            for f, row in enumerate(KEPT):
                send_ref[p, f] = tmp_ref[i, pl.ds(row, SLOTS, stride=8), :].astype(BF16)

        @pl.when(o > 0)
        def _():
            here.send_group(o - 1, send_flux)

        return carry

    lax.fori_loop(0, 16, pack, 0)
    own_rows = pltpu.make_async_copy(
        srow_ref.at[here.me, pl.ds(0, 1)], rrow_ref.at[here.me, pl.ds(0, 1)], own_sem.at[0]
    )
    own_rows.start()
    here.send_group(15, send_flux)
    own_flux = pltpu.make_async_copy(send_ref.at[here.me], got_ref.at[here.me], own_sem.at[1])
    own_flux.start()

    class Ring:
        def __init__(self, index, east, west, north, south):
            self.index, self.pairs = index, (east, west, north, south)

        def start(self):
            targets = (here.east, here.west, here.north, here.south)
            for d, ((src, dst), target) in enumerate(zip(self.pairs, targets)):
                whole = pl.ds(0, src.shape[0])
                pltpu.make_async_remote_copy(
                    src.at[whole], dst.at[whole], side_send.at[self.index * 4 + d],
                    side_recv.at[self.index * 4 + d], device_id=target, device_id_type=MESH,
                ).start()

        def wait(self):
            for d, (src, dst) in enumerate(self.pairs):
                whole = pl.ds(0, src.shape[0])
                at = self.index * 4 + d
                pltpu.make_async_copy(src.at[whole], src.at[whole], side_send.at[at]).wait()
                pltpu.make_async_copy(dst.at[whole], dst.at[whole], side_recv.at[at]).wait()

    lane = lax.broadcasted_iota(I32, (LANES, LANES), 1)

    def edge_columns(tile, j, to_east, to_west):
        to_east[...] = jnp.where(lane == j, pltpu.roll(tile, (j + 1) % LANES, 1), to_east[...])
        to_west[...] = jnp.where(lane == j, pltpu.roll(tile, j, 1), to_west[...])

    wet_ref[...] = jnp.zeros_like(wet_ref)
    wet_ref[inner, :] = land_ref[...].astype(F32)
    q_copy.wait()
    uv_copy.wait()

    def edges(l, carry):
        for t in range(2):
            j = t * levels + l
            edge_columns(q_ref[t, l, inner, :], j, pe_ref, pw_ref)
            pn_ref[pl.ds(j, 1), :] = q_ref[t, l, LANES + 7 : LANES + 8, :]
            ps_ref[pl.ds(j, 1), :] = q_ref[t, l, 8:9, :]
        j = 2 * levels + l
        edge_columns(uv_ref[0, l, inner, :], j, pe_ref, pw_ref)
        pn_ref[pl.ds(j, 1), :] = uv_ref[1, l, LANES + 7 : LANES + 8, :]
        ps_ref[pl.ds(j, 1), :] = uv_ref[1, l, 8:9, :]
        return carry

    for l in range(levels):
        edges(l, 0)
    jw = 3 * levels
    edge_columns(wet_ref[inner, :], jw, pe_ref, pw_ref)
    pn_ref[jw : jw + 1, :] = wet_ref[LANES + 7 : LANES + 8, :]
    ps_ref[jw : jw + 1, :] = wet_ref[8:9, :]
    inputs_ring = Ring(
        0, (pe_ref, hw_ref), (pw_ref, he_ref), (pn_ref, hs_ref), (ps_ref, hn_ref)
    )
    inputs_ring.start()

    own_rows.wait()
    wait_others(srow_ref, a2a_send.at[0], 1)
    wait_others(rrow_ref, a2a_recv.at[0], 1)
    rows = rrow_ref[:, 0:1, :].reshape(DEVICES, LANES).astype(BF16)
    upright = lax.broadcasted_iota(I32, (LANES, LANES), 0)
    ones = jnp.ones((LANES, LANES), BF16)

    def one_hot(b, carry):
        pick = (lane == b * 8 + upright // SLOTS).astype(F32).astype(BF16)
        spread = jnp.dot(pick, rows, preferred_element_type=F32)
        mine = jnp.where(lane == upright % SLOTS, spread, 0.0).astype(BF16)
        down = jnp.dot(mine, ones, preferred_element_type=F32)
        across = lax.dot_general(
            ones, mine, (((1,), (1,)), ((), ())), preferred_element_type=F32
        )
        at = slice(b * LANES, (b + 1) * LANES)
        hott_ref[at, :] = (down == lane.astype(F32)).astype(F32).astype(BF16)
        hot_ref[:, at] = (across == upright.astype(F32)).astype(F32).astype(BF16)
        return carry

    for b in range(SLOTS):
        one_hot(b, 0)
    blocks = temp_ref.shape[0]
    srchot_ref[...] = (
        (lax.broadcasted_iota(I32, (blocks, nonzeros), 0) == srcrow_ref[...])
        .astype(F32)
        .astype(BF16)
    )

    inputs_ring.wait()
    inside_e = jnp.where(here.gy < 7, 1.0, 0.0)
    inside_w = jnp.where(here.gy > 0, 1.0, 0.0)
    inside_n = jnp.where(here.band < 15, 1.0, 0.0)
    inside_s = jnp.where(here.band > 0, 1.0, 0.0)
    wet_ref[LANES + 8 : LANES + 9, :] = hn_ref[jw : jw + 1, :] * inside_n
    wet_ref[7:8, :] = hs_ref[jw : jw + 1, :] * inside_s
    slane = lax.broadcasted_iota(I32, (STRIP, LANES), 1)
    strips = range(0, LANES, STRIP)

    def to_last(ref, r, j):
        return pltpu.roll(ref[r : r + STRIP, :], (2 * LANES - 1 - j) % LANES, 1)

    def to_first(ref, r, j):
        return pltpu.roll(ref[r : r + STRIP, :], (LANES - j) % LANES, 1)

    def east_west(tile, east, west):
        return (
            jnp.where(slane == LANES - 1, east, pltpu.roll(tile, LANES - 1, 1)),
            jnp.where(slane == 0, west, pltpu.roll(tile, 1, 1)),
        )

    for r in strips:
        wet = wet_ref[8 + r : 8 + r + STRIP, :]
        east, west = east_west(
            wet, to_last(he_ref, r, jw) * inside_e, to_first(hw_ref, r, jw) * inside_w
        )
        open_ref[0, r : r + STRIP, :] = wet * east
        open_ref[1, r : r + STRIP, :] = wet * west
        open_ref[2, r : r + STRIP, :] = wet * wet_ref[9 + r : 9 + r + STRIP, :]
        open_ref[3, r : r + STRIP, :] = wet * wet_ref[7 + r : 7 + r + STRIP, :]

    def coefficients(l):
        j = 2 * levels + l
        uv_ref[1, l, LANES + 8 : LANES + 9, :] = hn_ref[pl.ds(j, 1), :]
        uv_ref[1, l, 7:8, :] = hs_ref[pl.ds(j, 1), :]
        for r in strips:
            at = slice(r, r + STRIP)
            u = uv_ref[0, l, 8 + r : 8 + r + STRIP, :]
            east, west = east_west(u, to_last(he_ref, r, j), to_first(hw_ref, r, j))
            v = uv_ref[1, l, 8 + r : 8 + r + STRIP, :]
            north = uv_ref[1, l, 9 + r : 9 + r + STRIP, :]
            south = uv_ref[1, l, 7 + r : 7 + r + STRIP, :]
            loss = 1.0 - 2.0 * KV * wet_ref[8 + r : 8 + r + STRIP, :]
            for d, (sign, beside, own) in enumerate(
                ((-1.0, east, u), (1.0, west, u), (-1.0, north, v), (1.0, south, v))
            ):
                gate = open_ref[d, at, :]
                flow = (0.25 * sign) * (own + beside) * gate
                coef_ref[d, l, at, :] = KH * gate + flow
                loss = loss - (KH * gate - flow)
            coef_ref[4, l, at, :] = loss

    def advance(ref, t, l, r, east, west):
        at = slice(r, r + STRIP)
        mid = slice(8 + r, 8 + r + STRIP)
        c = ref[t, l, mid, :]
        east, west = east_west(c, east, west)
        fixed = isinstance(l, int)
        above = c if fixed and l == 0 else ref[t, l - 1, mid, :]
        below = c if fixed and l == levels - 1 else ref[t, l + 1, mid, :]
        return (
            coef_ref[4, l, at, :] * c
            + coef_ref[0, l, at, :] * east
            + coef_ref[1, l, at, :] * west
            + coef_ref[2, l, at, :] * ref[t, l, 9 + r : 9 + r + STRIP, :]
            + coef_ref[3, l, at, :] * ref[t, l, 7 + r : 7 + r + STRIP, :]
            + (KV * wet_ref[mid, :]) * (above + below)
        )

    def set_rows(ref, t, l, north, south):
        ref[t, l, LANES + 8 : LANES + 9, :] = north
        ref[t, l, 7:8, :] = south

    def first_step(l, carry):
        coefficients(l)
        for t in range(2):
            j = t * levels + l
            set_rows(q_ref, t, l, hn_ref[pl.ds(j, 1), :], hs_ref[pl.ds(j, 1), :])
            for r in strips:
                q1_ref[t, l, 8 + r : 8 + r + STRIP, :] = advance(
                    q_ref, t, l, r, to_last(he_ref, r, j), to_first(hw_ref, r, j)
                )
        return carry

    lax.fori_loop(1, levels - 1, first_step, 0)
    first_step(levels - 1, 0)

    own_flux.wait()
    wait_others(got_ref, a2a_recv.at[1], CAP)
    for f in range(0, len(KEPT), 2):
        fields = [
            got_ref[:, g].reshape(DEVICES * SLOTS, LANES)
            for g in range(f, min(f + 2, len(KEPT)))
        ]
        total = jnp.dot(
            hot_ref[...], jnp.concatenate(fields, axis=1), preferred_element_type=F32
        )
        for i in range(len(fields)):
            flux_ref[f + i] = total[:, i * LANES : (i + 1) * LANES]
    flux_ring = Ring(
        1, (flux_ref.at[3], hwu_ref), (flux_ref.at[3], heu_ref),
        (flux_ref.at[4, pl.ds(LANES - 8, 8)], hsv_ref), (flux_ref.at[4, pl.ds(0, 8)], hnv_ref),
    )
    flux_ring.start()
    wait_others(send_ref, a2a_send.at[1], CAP)
    heat_scale = 0.3 * (1.0 - DECAY)

    def warmed(t, l, r, scale):
        at, mid = slice(r, r + STRIP), slice(8 + r, 8 + r + STRIP)
        q1_ref[t, l, mid, :] = q1_ref[t, l, mid, :] + wet_ref[mid, :] * (
            scale * flux_ref[0, at, :]
        )

    for r in strips:
        at, mid = slice(r, r + STRIP), slice(8 + r, 8 + r + STRIP)
        uv_ref[0, 0, mid, :] = uv_ref[0, 0, mid, :] + 0.1 * flux_ref[3, at, :]
        uv_ref[1, 0, mid, :] = uv_ref[1, 0, mid, :] + 0.1 * flux_ref[4, at, :]
        warmed(0, 1, r, heat_scale * DECAY)
    for t in range(2):
        j = t * levels
        set_rows(q_ref, t, 0, hn_ref[j : j + 1, :], hs_ref[j : j + 1, :])
    flux_ring.wait()
    ju = 2 * levels
    he_ref[...] = he_ref[...] + jnp.where(lane == ju, 0.1 * pltpu.roll(heu_ref[...], ju, 1), 0.0)
    hw_ref[...] = hw_ref[...] + jnp.where(
        lane == ju, 0.1 * pltpu.roll(hwu_ref[...], ju + 1, 1), 0.0
    )
    hn_ref[ju : ju + 1, :] = hn_ref[ju : ju + 1, :] + 0.1 * hnv_ref[0:1, :]
    hs_ref[ju : ju + 1, :] = hs_ref[ju : ju + 1, :] + 0.1 * hsv_ref[7:8, :]
    coefficients(0)

    def surface(t, r):
        at = slice(r, r + STRIP)
        if t == 0:
            force = heat_scale * flux_ref[0, at, :] + 0.2 * flux_ref[1, at, :]
        else:
            force = 0.2 * flux_ref[2, at, :]
        return wet_ref[8 + r : 8 + r + STRIP, :] * force

    def surface_step(t):
        j = t * levels
        for r in strips:
            q1_ref[t, 0, 8 + r : 8 + r + STRIP, :] = advance(
                q_ref, t, 0, r, to_last(he_ref, r, j), to_first(hw_ref, r, j)
            ) + surface(t, r)

    surface_step(0)
    top_ring = Ring(
        2, (q1_ref.at[0, 0, inner], hw1_ref), (q1_ref.at[0, 0, inner], he1_ref),
        (q1_ref.at[0, 0, pl.ds(LANES, 8)], hs1_ref), (q1_ref.at[0, 0, pl.ds(8, 8)], hn1_ref),
    )
    top_ring.start()
    surface_step(1)

    def forced(l, scale):
        for r in strips:
            warmed(0, l, r, scale)
        return scale * DECAY

    lax.fori_loop(2, levels, forced, jnp.float32(heat_scale * DECAY * DECAY))

    def edges_again(l, carry):
        for t in range(2):
            j = t * levels + l
            edge_columns(q1_ref[t, l, inner, :], j, pe2_ref, pw2_ref)
            pn2_ref[pl.ds(j, 1), :] = q1_ref[t, l, LANES + 7 : LANES + 8, :]
            ps2_ref[pl.ds(j, 1), :] = q1_ref[t, l, 8:9, :]
        return carry

    top_ring.wait()
    set_rows(q1_ref, 0, 0, hn1_ref[0:1, :], hs1_ref[7:8, :])
    for r in strips:
        q2_ref[0, 0, r : r + STRIP, :] = advance(
            q1_ref, 0, 0, r, to_last(he1_ref, r, 0), to_first(hw1_ref, r, LANES - 1)
        ) + surface(0, r)

    sst = q2_ref[0, 0].astype(BF16)

    def select(b, carry):
        at = pl.ds(pl.multiple_of(b * LANES, LANES), LANES)
        picked = jnp.dot(hott_ref[at, :], sst, preferred_element_type=F32).astype(BF16)
        sret_ref[pl.ds(b * 8, 8)] = picked.reshape(8, SLOTS, LANES)
        return carry

    lax.fori_loop(0, SLOTS, select, 0)
    here.each(all_to_all(2, sret_ref, ret_ref, lambda ref, i: ref.at[i, pl.ds(0, CAP)]))
    own_ret = pltpu.make_async_copy(sret_ref.at[here.me], ret_ref.at[here.me], own_sem.at[2])
    own_ret.start()

    for l in range(levels):
        edges_again(l, 0)
    last_ring = Ring(
        3, (pe2_ref, hw2_ref), (pw2_ref, he2_ref), (pn2_ref, hs2_ref), (ps2_ref, hn2_ref)
    )
    last_ring.start()
    last_ring.wait()

    def second(t, l, r):
        j = t * levels + l
        return advance(q1_ref, t, l, r, to_last(he2_ref, r, j), to_first(hw2_ref, r, j))

    def rows_of(t, l):
        j = t * levels + l
        set_rows(q1_ref, t, l, hn2_ref[pl.ds(j, 1), :], hs2_ref[pl.ds(j, 1), :])

    rows_of(1, 0)
    for r in strips:
        q2_ref[1, 0, r : r + STRIP, :] = second(1, 0, r) + surface(1, r)

    def second_step(l, scale):
        for t in range(2):
            rows_of(t, l)
            for r in strips:
                fresh = second(t, l, r)
                if t == 0:
                    fresh = fresh + wet_ref[8 + r : 8 + r + STRIP, :] * (
                        scale * flux_ref[0, r : r + STRIP, :]
                    )
                q2_ref[t, l, r : r + STRIP, :] = fresh
        return scale * DECAY

    scale = lax.fori_loop(1, levels - 1, second_step, jnp.float32(heat_scale * DECAY))
    second_step(levels - 1, scale)
    out_copy = pltpu.make_async_copy(q2_ref, out_hbm, out_sem)
    out_copy.start()

    own_ret.wait()
    wait_others(sret_ref, a2a_send.at[2], CAP)
    wait_others(ret_ref, a2a_recv.at[2], CAP)
    ret32_ref[pl.ds(0, DEVICES * SLOTS), :] = ret_ref[...].astype(F32).reshape(DEVICES * SLOTS, LANES)

    def backward(c, carry):
        for g in range(0, CHUNK, 8):
            base = c * CHUNK + g
            picked = jnp.concatenate(
                [ret32_ref[pl.ds(slot_ref[base + i], 1), :] for i in range(8)], axis=0
            )
            left = jnp.concatenate(
                [jnp.where(sub == i, picked, 0.0).astype(BF16) for i in range(8)], axis=1
            )
            right = w_ref[pl.ds(base, 8)].reshape(8 * LANES, LANES)
            terms_ref[pl.ds(pl.multiple_of(base, 8), 8), :] = jnp.dot(
                left, right, preferred_element_type=F32
            )
        return carry

    lax.fori_loop(0, chunks, backward, 0)
    terms = terms_ref[...]
    high = terms.astype(BF16)
    low = (terms - high.astype(F32)).astype(BF16)
    temp_ref[...] = jnp.dot(srchot_ref[...], high, preferred_element_type=F32) + jnp.dot(
        srchot_ref[...], low, preferred_element_type=F32
    )
    out_copy.wait()


def on_device(
    atm_flux, remap_weights, remap_src, remap_dst, remap_owner, tracers, currents, land_sea
):
    nonzeros, width = remap_weights.shape[0], remap_weights.shape[1]
    atm_blocks = atm_flux.shape[0]
    levels = tracers.shape[1]
    chunks = nonzeros // CHUNK

    owners = remap_owner[:, 0]
    hot = (owners[:, None] == jnp.arange(DEVICES, dtype=I32)[None, :]).astype(BF16)
    order = jnp.arange(nonzeros, dtype=I32)
    before = (order[:, None] > order[None, :]).astype(BF16)
    earlier = jnp.dot(before, hot, preferred_element_type=F32)
    position = jnp.sum(earlier * hot.astype(F32), axis=1).astype(I32)
    slot = owners * CAP + position
    taken = jnp.arange(DEVICES * CAP, dtype=I32)[:, None] == slot[None, :]
    kidx = jnp.sum(jnp.where(taken, order[None, :] - nonzeros, 0), axis=1) + nonzeros
    slot_rows = jnp.sum(jnp.where(taken, remap_dst[None, :] - 200, 0), axis=1) + 200
    row_table = jnp.pad(
        slot_rows.reshape(DEVICES, CAP).astype(F32), ((0, 0), (0, LANES - CAP)),
        constant_values=200.0,
    )

    vmem = pl.BlockSpec(memory_space=pltpu.VMEM)
    smem = pl.BlockSpec(memory_space=pltpu.SMEM)
    anywhere = pl.BlockSpec(memory_space=pl.ANY)
    padded = (2, levels, LANES + 16, LANES)
    tile = (LANES, LANES)
    scratch = [
        (remap_weights.shape, BF16), ((nonzeros + 1, 8, LANES), F32), ((8, SLOTS * 8, LANES), F32),
        ((DEVICES, len(KEPT), SLOTS, width), BF16), ((DEVICES, len(KEPT), SLOTS, width), BF16),
        ((DEVICES, 8, LANES), F32), ((DEVICES, 8, LANES), F32),
        ((LANES, DEVICES * SLOTS), BF16), ((DEVICES * SLOTS, LANES), BF16),
        ((len(KEPT),) + tile, F32),
        ((DEVICES, SLOTS, width), BF16), ((DEVICES, SLOTS, width), BF16),
        ((DEVICES * SLOTS + 8, width), F32), ((nonzeros, width), F32), ((atm_blocks, nonzeros), BF16),
        (padded, F32), (padded, F32), (padded, F32), (tracers.shape, F32),
        ((5, levels) + tile, F32), ((4,) + tile, F32), ((LANES + 16, LANES), F32),
        (tile, F32), (tile, F32), (tile, F32), (tile, F32),
        (tile, F32), (tile, F32), (tile, F32), (tile, F32),
        (tile, F32), (tile, F32), ((8, LANES), F32), ((8, LANES), F32),
        (tile, F32), (tile, F32), ((8, LANES), F32), ((8, LANES), F32),
        (tile, F32), (tile, F32), (tile, F32), (tile, F32),
        (tile, F32), (tile, F32), (tile, F32), (tile, F32),
    ]
    return pl.pallas_call(
        coupled_kernel,
        name="coupled",
        out_shape=[
            jax.ShapeDtypeStruct(tracers.shape, F32),
            jax.ShapeDtypeStruct((atm_blocks, width), F32),
        ],
        in_specs=[smem, smem, smem, vmem, vmem, vmem, vmem, anywhere, anywhere, anywhere],
        out_specs=[anywhere, vmem],
        scratch_shapes=[pltpu.VMEM(shape, kind) for shape, kind in scratch]
        + [
            pltpu.SemaphoreType.DMA((chunks,)),
            pltpu.SemaphoreType.DMA((2,)),
            pltpu.SemaphoreType.DMA((3,)),
            pltpu.SemaphoreType.DMA((3,)),
            pltpu.SemaphoreType.DMA((16,)),
            pltpu.SemaphoreType.DMA((16,)),
            pltpu.SemaphoreType.DMA((3,)),
            pltpu.SemaphoreType.DMA,
        ],
        compiler_params=pltpu.CompilerParams(
            collective_id=0, has_side_effects=True, vmem_limit_bytes=64000 * 1024
        ),
    )(
        remap_src, kidx, owners * SLOTS + position, row_table, remap_src[None, :], atm_flux,
        land_sea, remap_weights, tracers, currents,
    )


def solution(mesh):
    tiles = P(None, None, ("sec", "gx"), "gy")
    shares = ("sec", "gx", "gy")

    def run(*args):
        return tuple(on_device(*args))

    return jax.shard_map(
        run,
        mesh=mesh,
        in_specs=(
            P(shares, None, None),
            P(shares, None, None),
            P(shares),
            P(shares),
            P(shares, None),
            tiles,
            tiles,
            P(("sec", "gx"), "gy"),
        ),
        out_specs=(tiles, P(shares, None)),
        check_vma=False,
    )
```

```python
import math

import jax
import jax.numpy as jnp
from jax import lax
from jax.experimental import pallas as pl
from jax.experimental.pallas import tpu as pltpu
from jax.sharding import PartitionSpec as P

KH = 0.1
KV = 0.1
CAP = 10
SLOTS = 16
KEPT = 5
TAIL = CAP - 8
ROWS = CAP * KEPT
LANES = 128
DEVICES = 128
CHUNK = 32
STRIP = 32
DECAY = math.exp(-0.25)
LOGICAL = pl.DeviceIdType.LOGICAL
MESH = pl.DeviceIdType.MESH
BF16 = jnp.bfloat16
F32 = jnp.float32
I32 = jnp.int32


class Torus:
    def __init__(self):
        sec, gx, gy = lax.axis_index("sec"), lax.axis_index("gx"), lax.axis_index("gy")
        self.band, self.gy = sec * 8 + gx, gy
        self.me = self.band * 8 + gy
        up, down = (self.band + 1) % 16, (self.band + 15) % 16
        self.north = (up // 8, up % 8, gy)
        self.south = (down // 8, down % 8, gy)
        self.east = (sec, gx, (gy + 1) % 8)
        self.west = (sec, gx, (gy + 7) % 8)
        self.y, self.z = (gy % 2) * 2 + sec, gx // 2
        self.xs = [((gy // 2 + d) % 4) * 2 for d in range(4)]
        self.cores = [((gx + d) % 2) * 8 for d in range(2)]

    def group(self, o):
        partners = []
        for d in (2, 1, 3, 0):
            y = (self.y + 3 - o % 4 + d) % 4
            z = (self.z + 3 - o // 4 + d) % 4
            base = (y % 2) * 64 + y // 2 + z * 16 + self.xs[d]
            partners += [base + self.cores[c] for c in (1, 0)]
        return partners

    def send_group(self, o, act):
        partners = self.group(o)
        for p in partners[:-1]:
            act(p)

        @pl.when(o < 15)
        def _():
            act(partners[-1])

    def each(self, act):
        def body(o, carry):
            self.send_group(o, act)
            return carry

        lax.fori_loop(0, 16, body, 0)


def wait_others(ref, sem, rows):
    first = pl.ds(0, DEVICES - 1)
    view = ref.at[first, pl.ds(0, rows)]
    pltpu.make_async_copy(view, view, sem).wait()


def coupled_kernel(
    src_ref, kidx_ref, slot_ref, row_ref, srcrow_ref, atm_ref, land_ref, w_hbm, q_hbm, uv_hbm,
    out_hbm, temp_ref,
    w_ref, part_ref, tmp_ref, send_ref, got_ref, srow_ref, rrow_ref, hot_ref, hott_ref, rest_ref,
    flux_ref, sret_ref, ret_ref, ret32_ref, terms_ref, srchot_ref,
    q_ref, uv_ref, q1_ref, q2_ref, coef_ref, open_ref, wet_ref,
    pe_ref, hx_ref, he_ref, hw_ref, pn_ref, ps_ref, hn_ref, hs_ref,
    heu_ref, hwu_ref, hnv_ref, hsv_ref,
    he1_ref, hw1_ref, hn1_ref, hs1_ref,
    pe2_ref, hx2_ref, he2_ref, hw2_ref, pn2_ref, ps2_ref, hn2_ref, hs2_ref,
    w_sem, in_sem, a2a_send, a2a_recv, side_send, side_recv, own_sem, out_sem,
):
    here = Torus()
    nonzeros = w_ref.shape[0]
    chunks = nonzeros // CHUNK
    levels = q_ref.shape[1]
    inner = pl.ds(8, LANES)

    def weight_copy(c):
        part = pl.ds(c * CHUNK, CHUNK)
        return pltpu.make_async_copy(w_hbm.at[part], w_ref.at[part], w_sem.at[c])

    def start_weights(c, carry):
        weight_copy(c).start()
        return carry

    lax.fori_loop(0, chunks, start_weights, 0)
    q_copy = pltpu.make_async_copy(q_hbm, q_ref.at[:, :, inner], in_sem.at[0])
    uv_copy = pltpu.make_async_copy(uv_hbm, uv_ref.at[:, :, inner], in_sem.at[1])
    q_copy.start()
    uv_copy.start()

    got_ref[...] = jnp.zeros_like(got_ref)
    barrier = pltpu.get_barrier_semaphore()
    here.each(
        lambda p: pl.semaphore_signal(barrier, inc=1, device_id=p, device_id_type=LOGICAL)
    )
    srow_ref[:, 0:1, :] = row_ref[...].reshape(DEVICES, 1, LANES)
    part_ref[nonzeros] = jnp.zeros((8, LANES), F32)
    pn_ref[...] = jnp.zeros_like(pn_ref)
    ps_ref[...] = jnp.zeros_like(ps_ref)
    pn2_ref[...] = jnp.zeros_like(pn2_ref)
    ps2_ref[...] = jnp.zeros_like(ps2_ref)

    sub = lax.broadcasted_iota(I32, (8, LANES), 0)
    takes = [
        jnp.where(sub < 2, 1.0, 0.0),
        jnp.where(sub == 1, 1.0, 0.0),
        jnp.where((sub == 1) | (sub == 2), 1.0, 0.0),
        jnp.where(sub == 2, -0.5, jnp.where((sub == 3) | (sub == 4), 1.0, 0.0)),
        jnp.where(sub == 1, -0.75, 0.0),
    ]
    blank = jnp.zeros((8, LANES), BF16)

    def combine(p):
        p = p.astype(BF16).astype(F32)
        total = p * takes[0]
        for up in range(1, 5):
            total = total + pltpu.roll(p, 8 - up, 0) * takes[up]
        return total

    def forward(c, carry):
        weight_copy(c).wait()
        for i in range(0, CHUNK, 2):
            k = c * CHUNK + i
            left = jnp.concatenate(
                [
                    jnp.concatenate([atm_ref[src_ref[k]], blank], axis=1),
                    jnp.concatenate([blank, atm_ref[src_ref[k + 1]]], axis=1),
                ],
                axis=0,
            )
            right = jnp.concatenate([w_ref[k], w_ref[k + 1]], axis=1)
            p = lax.dot_general(
                left, right, (((1,), (1,)), ((), ())), preferred_element_type=F32
            )
            part_ref[k] = combine(p[:8])
            part_ref[k + 1] = combine(p[8:])
        return carry

    def all_to_all(index, src, dst, cut):
        def act(p):
            pltpu.make_async_remote_copy(
                cut(src, p), cut(dst, here.me), a2a_send.at[index], a2a_recv.at[index],
                device_id=p, device_id_type=LOGICAL,
            ).start()

        return act

    lax.fori_loop(0, chunks // 2, forward, 0)
    pl.semaphore_wait(barrier, DEVICES - 1)
    here.each(all_to_all(0, srow_ref, rrow_ref, lambda ref, i: ref.at[i, pl.ds(0, 1)]))
    lax.fori_loop(chunks // 2, chunks, forward, 0)
    send_flux = all_to_all(1, send_ref, got_ref, lambda ref, i: ref.at[i, pl.ds(0, ROWS)])

    def pack(o, carry):
        partners = here.group(o)
        for i, p in enumerate(partners):
            found = [part_ref[kidx_ref[p * CAP + s]] for s in range(CAP)]
            for s in range(8):
                tmp_ref[i, s * 8 : s * 8 + 8, :] = found[s]
            shifted = pltpu.roll(found[9], KEPT, 0)
            send_ref[p, 40:48] = jnp.where(sub < KEPT, found[8], shifted).astype(BF16)
            send_ref[p, 48:56] = shifted.astype(BF16)
        for i, p in enumerate(partners):
            for f in range(KEPT):
                send_ref[p, f * 8 : f * 8 + 8] = tmp_ref[
                    i, pl.ds(f, 8, stride=8), :
                ].astype(BF16)

        @pl.when(o > 0)
        def _():
            here.send_group(o - 1, send_flux)

        return carry

    lax.fori_loop(0, 16, pack, 0)
    own_rows = pltpu.make_async_copy(
        srow_ref.at[here.me, pl.ds(0, 1)], rrow_ref.at[here.me, pl.ds(0, 1)], own_sem.at[0]
    )
    own_rows.start()
    here.send_group(15, send_flux)
    own_flux = pltpu.make_async_copy(send_ref.at[here.me], got_ref.at[here.me], own_sem.at[1])
    own_flux.start()

    class Ring:
        def __init__(self, index, east, west, north, south):
            self.index, self.pairs = index, (east, west, north, south)

        def start(self):
            targets = (here.east, here.west, here.north, here.south)
            for d, ((src, dst), target) in enumerate(zip(self.pairs, targets)):
                whole = pl.ds(0, src.shape[0])
                pltpu.make_async_remote_copy(
                    src.at[whole], dst.at[whole], side_send.at[self.index * 4 + d],
                    side_recv.at[self.index * 4 + d], device_id=target, device_id_type=MESH,
                ).start()

        def wait(self):
            for d, (src, dst) in enumerate(self.pairs):
                whole = pl.ds(0, src.shape[0])
                at = self.index * 4 + d
                pltpu.make_async_copy(src.at[whole], src.at[whole], side_send.at[at]).wait()
                pltpu.make_async_copy(dst.at[whole], dst.at[whole], side_recv.at[at]).wait()

    lane = lax.broadcasted_iota(I32, (LANES, LANES), 1)

    slane = lax.broadcasted_iota(I32, (STRIP, LANES), 1)
    pair = slane // 2
    strips = range(0, LANES, STRIP)

    def pack_columns(tiles, out_ref):
        for r in strips:
            packed = jnp.zeros((STRIP, LANES), F32)
            for i, tile in enumerate(tiles):
                packed = jnp.where(pair == i, pltpu.roll(tile(r), 2 * i + 1, 1), packed)
            out_ref[r : r + STRIP, :] = packed

    def join_columns(east_ref, west_ref, out_ref):
        for r in strips:
            at = slice(r, r + STRIP)
            out_ref[at, :] = jnp.where(
                slane % 2 == 0, pltpu.roll(east_ref[at, :], LANES - 1, 1),
                pltpu.roll(west_ref[at, :], 1, 1),
            )

    def strip_of(ref, *lead):
        return lambda r: ref[(*lead, slice(8 + r, 8 + r + STRIP), slice(None))]

    wet_ref[...] = jnp.zeros_like(wet_ref)
    wet_ref[inner, :] = land_ref[...].astype(F32)
    q_copy.wait()
    uv_copy.wait()

    jw = 3 * levels
    pack_columns(
        [strip_of(q_ref, t, l) for t in range(2) for l in range(levels)]
        + [strip_of(uv_ref, 0, l) for l in range(levels)]
        + [strip_of(wet_ref)],
        pe_ref,
    )
    for l in range(levels):
        for t in range(2):
            j = t * levels + l
            pn_ref[j : j + 1, :] = q_ref[t, l, LANES + 7 : LANES + 8, :]
            ps_ref[j : j + 1, :] = q_ref[t, l, 8:9, :]
        j = 2 * levels + l
        pn_ref[j : j + 1, :] = uv_ref[1, l, LANES + 7 : LANES + 8, :]
        ps_ref[j : j + 1, :] = uv_ref[1, l, 8:9, :]
    pn_ref[jw : jw + 1, :] = wet_ref[LANES + 7 : LANES + 8, :]
    ps_ref[jw : jw + 1, :] = wet_ref[8:9, :]
    inputs_ring = Ring(
        0, (pe_ref, hw_ref), (pe_ref, he_ref), (pn_ref, hs_ref), (ps_ref, hn_ref)
    )
    inputs_ring.start()

    own_rows.wait()
    wait_others(srow_ref, a2a_send.at[0], 1)
    wait_others(rrow_ref, a2a_recv.at[0], 1)
    rows = rrow_ref[:, 0:1, :].reshape(DEVICES, LANES).astype(BF16)
    upright = lax.broadcasted_iota(I32, (LANES, LANES), 0)
    ones = jnp.ones((LANES, LANES), BF16)

    def spread_rows(b, each):
        pick = (lane == b * (LANES // each) + upright // each).astype(F32).astype(BF16)
        spread = jnp.dot(pick, rows, preferred_element_type=F32)
        return jnp.where(lane == upright % each, spread, 0.0).astype(BF16)

    for b in range(SLOTS):
        down = jnp.dot(spread_rows(b, SLOTS), ones, preferred_element_type=F32)
        hott_ref[b * LANES : (b + 1) * LANES, :] = (
            (down == lane.astype(F32)).astype(F32).astype(BF16)
        )
    for b in range(8):
        across = lax.dot_general(
            ones, spread_rows(b, 8), (((1,), (1,)), ((), ())), preferred_element_type=F32
        )
        hot_ref[:, b * LANES : (b + 1) * LANES] = (
            (across == upright.astype(F32)).astype(F32).astype(BF16)
        )
    turned = jnp.transpose(rrow_ref[:, 0:1, :].reshape(DEVICES, LANES))
    for i in range(TAIL):
        hot_ref[:, (8 + i) * LANES : (9 + i) * LANES] = (
            (turned[8 + i : 9 + i, :] == upright.astype(F32)).astype(F32).astype(BF16)
        )
    blocks = temp_ref.shape[0]
    srchot_ref[...] = (
        (lax.broadcasted_iota(I32, (blocks, nonzeros), 0) == srcrow_ref[...])
        .astype(F32)
        .astype(BF16)
    )

    inputs_ring.wait()
    inside_e = jnp.where(here.gy < 7, 1.0, 0.0)
    inside_w = jnp.where(here.gy > 0, 1.0, 0.0)
    inside_n = jnp.where(here.band < 15, 1.0, 0.0)
    inside_s = jnp.where(here.band > 0, 1.0, 0.0)
    wet_ref[LANES + 8 : LANES + 9, :] = hn_ref[jw : jw + 1, :] * inside_n
    wet_ref[7:8, :] = hs_ref[jw : jw + 1, :] * inside_s
    join_columns(he_ref, hw_ref, hx_ref)

    def columns_by(ref, r, i):
        return pltpu.roll(ref[r : r + STRIP, :], LANES - 1 - 2 * i, 1)

    def east_west(tile, both):
        return (
            jnp.where(slane == LANES - 1, both, pltpu.roll(tile, LANES - 1, 1)),
            jnp.where(slane == 0, both, pltpu.roll(tile, 1, 1)),
        )

    for r in strips:
        wet = wet_ref[8 + r : 8 + r + STRIP, :]
        both = columns_by(hx_ref, r, jw)
        east, west = east_west(wet, jnp.where(slane == 0, both * inside_w, both * inside_e))
        open_ref[0, r : r + STRIP, :] = wet * east
        open_ref[1, r : r + STRIP, :] = wet * west
        open_ref[2, r : r + STRIP, :] = wet * wet_ref[9 + r : 9 + r + STRIP, :]
        open_ref[3, r : r + STRIP, :] = wet * wet_ref[7 + r : 7 + r + STRIP, :]

    def coefficients(l):
        j = 2 * levels + l
        uv_ref[1, l, LANES + 8 : LANES + 9, :] = hn_ref[pl.ds(j, 1), :]
        uv_ref[1, l, 7:8, :] = hs_ref[pl.ds(j, 1), :]
        for r in strips:
            at = slice(r, r + STRIP)
            u = uv_ref[0, l, 8 + r : 8 + r + STRIP, :]
            east, west = east_west(u, columns_by(hx_ref, r, j))
            v = uv_ref[1, l, 8 + r : 8 + r + STRIP, :]
            north = uv_ref[1, l, 9 + r : 9 + r + STRIP, :]
            south = uv_ref[1, l, 7 + r : 7 + r + STRIP, :]
            loss = 1.0 - 2.0 * KV * wet_ref[8 + r : 8 + r + STRIP, :]
            for d, (sign, beside, own) in enumerate(
                ((-1.0, east, u), (1.0, west, u), (-1.0, north, v), (1.0, south, v))
            ):
                gate = open_ref[d, at, :]
                flow = (0.25 * sign) * (own + beside) * gate
                coef_ref[d, l, at, :] = KH * gate + flow
                loss = loss - (KH * gate - flow)
            coef_ref[4, l, at, :] = loss

    def advance(ref, t, l, r, both):
        at = slice(r, r + STRIP)
        mid = slice(8 + r, 8 + r + STRIP)
        c = ref[t, l, mid, :]
        east, west = east_west(c, both)
        fixed = isinstance(l, int)
        above = c if fixed and l == 0 else ref[t, l - 1, mid, :]
        below = c if fixed and l == levels - 1 else ref[t, l + 1, mid, :]
        return (
            coef_ref[4, l, at, :] * c
            + coef_ref[0, l, at, :] * east
            + coef_ref[1, l, at, :] * west
            + coef_ref[2, l, at, :] * ref[t, l, 9 + r : 9 + r + STRIP, :]
            + coef_ref[3, l, at, :] * ref[t, l, 7 + r : 7 + r + STRIP, :]
            + (KV * wet_ref[mid, :]) * (above + below)
        )

    def set_rows(ref, t, l, north, south):
        ref[t, l, LANES + 8 : LANES + 9, :] = north
        ref[t, l, 7:8, :] = south

    def first_step(l, carry):
        coefficients(l)
        for t in range(2):
            j = t * levels + l
            set_rows(q_ref, t, l, hn_ref[pl.ds(j, 1), :], hs_ref[pl.ds(j, 1), :])
            for r in strips:
                q1_ref[t, l, 8 + r : 8 + r + STRIP, :] = advance(
                    q_ref, t, l, r, columns_by(hx_ref, r, j)
                )
        return carry

    lax.fori_loop(1, levels - 1, first_step, 0)
    first_step(levels - 1, 0)

    own_flux.wait()
    wait_others(got_ref, a2a_recv.at[1], ROWS)
    rest_ref[...] = got_ref[:, 40:56, :].astype(F32).reshape(DEVICES * SLOTS, LANES)

    def field(f):
        body = got_ref[:, f * 8 : f * 8 + 8, :].astype(F32).reshape(DEVICES * 8, LANES)
        tails = [
            rest_ref[pl.ds(i * KEPT + f, DEVICES, stride=SLOTS), :] for i in range(TAIL)
        ]
        return jnp.concatenate([body] + tails, axis=0).astype(BF16)

    for f in range(0, KEPT, 2):
        fields = [field(g) for g in range(f, min(f + 2, KEPT))]
        total = jnp.dot(
            hot_ref[...], jnp.concatenate(fields, axis=1), preferred_element_type=F32
        )
        for i in range(len(fields)):
            flux_ref[f + i] = total[:, i * LANES : (i + 1) * LANES]
    flux_ring = Ring(
        1, (flux_ref.at[3], hwu_ref), (flux_ref.at[3], heu_ref),
        (flux_ref.at[4, pl.ds(LANES - 8, 8)], hsv_ref), (flux_ref.at[4, pl.ds(0, 8)], hnv_ref),
    )
    flux_ring.start()
    wait_others(send_ref, a2a_send.at[1], ROWS)
    heat_scale = 0.3 * (1.0 - DECAY)

    def warmed(t, l, r, scale):
        at, mid = slice(r, r + STRIP), slice(8 + r, 8 + r + STRIP)
        q1_ref[t, l, mid, :] = q1_ref[t, l, mid, :] + wet_ref[mid, :] * (
            scale * flux_ref[0, at, :]
        )

    for r in strips:
        at, mid = slice(r, r + STRIP), slice(8 + r, 8 + r + STRIP)
        uv_ref[0, 0, mid, :] = uv_ref[0, 0, mid, :] + 0.1 * flux_ref[3, at, :]
        uv_ref[1, 0, mid, :] = uv_ref[1, 0, mid, :] + 0.1 * flux_ref[4, at, :]
        warmed(0, 1, r, heat_scale * DECAY)
    for t in range(2):
        j = t * levels
        set_rows(q_ref, t, 0, hn_ref[j : j + 1, :], hs_ref[j : j + 1, :])
    flux_ring.wait()
    ju = 2 * levels
    hx_ref[...] = hx_ref[...] + 0.1 * jnp.where(
        lane == 2 * ju, pltpu.roll(heu_ref[...], 2 * ju, 1),
        jnp.where(lane == 2 * ju + 1, pltpu.roll(hwu_ref[...], 2 * ju + 2, 1), 0.0),
    )
    hn_ref[ju : ju + 1, :] = hn_ref[ju : ju + 1, :] + 0.1 * hnv_ref[0:1, :]
    hs_ref[ju : ju + 1, :] = hs_ref[ju : ju + 1, :] + 0.1 * hsv_ref[7:8, :]
    coefficients(0)

    def surface(t, r):
        at = slice(r, r + STRIP)
        if t == 0:
            force = heat_scale * flux_ref[0, at, :] + 0.2 * flux_ref[1, at, :]
        else:
            force = 0.2 * flux_ref[2, at, :]
        return wet_ref[8 + r : 8 + r + STRIP, :] * force

    def surface_step(t):
        j = t * levels
        for r in strips:
            q1_ref[t, 0, 8 + r : 8 + r + STRIP, :] = advance(
                q_ref, t, 0, r, columns_by(hx_ref, r, j)
            ) + surface(t, r)

    surface_step(0)
    top_ring = Ring(
        2, (q1_ref.at[0, 0, inner], hw1_ref), (q1_ref.at[0, 0, inner], he1_ref),
        (q1_ref.at[0, 0, pl.ds(LANES, 8)], hs1_ref), (q1_ref.at[0, 0, pl.ds(8, 8)], hn1_ref),
    )
    top_ring.start()
    surface_step(1)

    def forced(l, scale):
        for r in strips:
            warmed(0, l, r, scale)
        return scale * DECAY

    lax.fori_loop(2, levels, forced, jnp.float32(heat_scale * DECAY * DECAY))

    top_ring.wait()
    set_rows(q1_ref, 0, 0, hn1_ref[0:1, :], hs1_ref[7:8, :])
    for r in strips:
        q2_ref[0, 0, r : r + STRIP, :] = advance(
            q1_ref, 0, 0, r,
            jnp.where(
                slane == 0, pltpu.roll(hw1_ref[r : r + STRIP, :], 1, 1),
                pltpu.roll(he1_ref[r : r + STRIP, :], LANES - 1, 1),
            ),
        ) + surface(0, r)

    sst = q2_ref[0, 0].astype(BF16)

    def select(b, carry):
        at = pl.ds(pl.multiple_of(b * LANES, LANES), LANES)
        picked = jnp.dot(hott_ref[at, :], sst, preferred_element_type=F32).astype(BF16)
        sret_ref[pl.ds(b * 8, 8)] = picked.reshape(8, SLOTS, LANES)
        return carry

    lax.fori_loop(0, SLOTS, select, 0)
    here.each(all_to_all(2, sret_ref, ret_ref, lambda ref, i: ref.at[i, pl.ds(0, CAP)]))
    own_ret = pltpu.make_async_copy(sret_ref.at[here.me], ret_ref.at[here.me], own_sem.at[2])
    own_ret.start()

    pack_columns([strip_of(q1_ref, t, l) for t in range(2) for l in range(levels)], pe2_ref)
    for l in range(levels):
        for t in range(2):
            j = t * levels + l
            pn2_ref[j : j + 1, :] = q1_ref[t, l, LANES + 7 : LANES + 8, :]
            ps2_ref[j : j + 1, :] = q1_ref[t, l, 8:9, :]
    last_ring = Ring(
        3, (pe2_ref, hw2_ref), (pe2_ref, he2_ref), (pn2_ref, hs2_ref), (ps2_ref, hn2_ref)
    )
    last_ring.start()
    last_ring.wait()
    join_columns(he2_ref, hw2_ref, hx2_ref)

    def second(t, l, r):
        j = t * levels + l
        return advance(q1_ref, t, l, r, columns_by(hx2_ref, r, j))

    def rows_of(t, l):
        j = t * levels + l
        set_rows(q1_ref, t, l, hn2_ref[pl.ds(j, 1), :], hs2_ref[pl.ds(j, 1), :])

    rows_of(1, 0)
    for r in strips:
        q2_ref[1, 0, r : r + STRIP, :] = second(1, 0, r) + surface(1, r)

    def second_step(l, scale):
        for t in range(2):
            rows_of(t, l)
            for r in strips:
                fresh = second(t, l, r)
                if t == 0:
                    fresh = fresh + wet_ref[8 + r : 8 + r + STRIP, :] * (
                        scale * flux_ref[0, r : r + STRIP, :]
                    )
                q2_ref[t, l, r : r + STRIP, :] = fresh
        return scale * DECAY

    scale = lax.fori_loop(1, levels - 1, second_step, jnp.float32(heat_scale * DECAY))
    second_step(levels - 1, scale)
    out_copy = pltpu.make_async_copy(q2_ref, out_hbm, out_sem)
    out_copy.start()

    own_ret.wait()
    wait_others(sret_ref, a2a_send.at[2], CAP)
    wait_others(ret_ref, a2a_recv.at[2], CAP)
    ret32_ref[pl.ds(0, DEVICES * SLOTS), :] = ret_ref[...].astype(F32).reshape(DEVICES * SLOTS, LANES)

    def backward(c, carry):
        for g in range(0, CHUNK, 8):
            base = c * CHUNK + g
            picked = jnp.concatenate(
                [ret32_ref[pl.ds(slot_ref[base + i], 1), :] for i in range(8)], axis=0
            )
            left = jnp.concatenate(
                [jnp.where(sub == i, picked, 0.0).astype(BF16) for i in range(8)], axis=1
            )
            right = w_ref[pl.ds(base, 8)].reshape(8 * LANES, LANES)
            terms_ref[pl.ds(pl.multiple_of(base, 8), 8), :] = jnp.dot(
                left, right, preferred_element_type=F32
            )
        return carry

    lax.fori_loop(0, chunks, backward, 0)
    terms = terms_ref[...]
    high = terms.astype(BF16)
    low = (terms - high.astype(F32)).astype(BF16)
    temp_ref[...] = jnp.dot(srchot_ref[...], high, preferred_element_type=F32) + jnp.dot(
        srchot_ref[...], low, preferred_element_type=F32
    )
    out_copy.wait()


def on_device(
    atm_flux, remap_weights, remap_src, remap_dst, remap_owner, tracers, currents, land_sea
):
    nonzeros, width = remap_weights.shape[0], remap_weights.shape[1]
    atm_blocks = atm_flux.shape[0]
    levels = tracers.shape[1]
    chunks = nonzeros // CHUNK

    owners = remap_owner[:, 0]
    hot = (owners[:, None] == jnp.arange(DEVICES, dtype=I32)[None, :]).astype(BF16)
    order = jnp.arange(nonzeros, dtype=I32)
    before = (order[:, None] > order[None, :]).astype(BF16)
    earlier = jnp.dot(before, hot, preferred_element_type=F32)
    position = jnp.sum(earlier * hot.astype(F32), axis=1).astype(I32)
    slot = owners * CAP + position
    taken = jnp.arange(DEVICES * CAP, dtype=I32)[:, None] == slot[None, :]
    kidx = jnp.sum(jnp.where(taken, order[None, :] - nonzeros, 0), axis=1) + nonzeros
    slot_rows = jnp.sum(jnp.where(taken, remap_dst[None, :] - 200, 0), axis=1) + 200
    row_table = jnp.pad(
        slot_rows.reshape(DEVICES, CAP).astype(F32), ((0, 0), (0, LANES - CAP)),
        constant_values=200.0,
    )

    vmem = pl.BlockSpec(memory_space=pltpu.VMEM)
    smem = pl.BlockSpec(memory_space=pltpu.SMEM)
    anywhere = pl.BlockSpec(memory_space=pl.ANY)
    padded = (2, levels, LANES + 16, LANES)
    tile = (LANES, LANES)
    scratch = [
        (remap_weights.shape, BF16), ((nonzeros + 1, 8, LANES), F32), ((8, 64, LANES), F32),
        ((DEVICES, 56, width), BF16), ((DEVICES, 56, width), BF16),
        ((DEVICES, 8, LANES), F32), ((DEVICES, 8, LANES), F32),
        ((LANES, DEVICES * CAP), BF16), ((DEVICES * SLOTS, LANES), BF16), ((DEVICES * SLOTS, LANES), F32),
        ((KEPT,) + tile, F32),
        ((DEVICES, SLOTS, width), BF16), ((DEVICES, SLOTS, width), BF16),
        ((DEVICES * SLOTS + 8, width), F32), ((nonzeros, width), F32), ((atm_blocks, nonzeros), BF16),
        (padded, F32), (padded, F32), (padded, F32), (tracers.shape, F32),
        ((5, levels) + tile, F32), ((4,) + tile, F32), ((LANES + 16, LANES), F32),
        (tile, F32), (tile, F32), (tile, F32), (tile, F32),
        (tile, F32), (tile, F32), (tile, F32), (tile, F32),
        (tile, F32), (tile, F32), ((8, LANES), F32), ((8, LANES), F32),
        (tile, F32), (tile, F32), ((8, LANES), F32), ((8, LANES), F32),
        (tile, F32), (tile, F32), (tile, F32), (tile, F32),
        (tile, F32), (tile, F32), (tile, F32), (tile, F32),
    ]
    return pl.pallas_call(
        coupled_kernel,
        name="coupled",
        out_shape=[
            jax.ShapeDtypeStruct(tracers.shape, F32),
            jax.ShapeDtypeStruct((atm_blocks, width), F32),
        ],
        in_specs=[smem, smem, smem, vmem, vmem, vmem, vmem, anywhere, anywhere, anywhere],
        out_specs=[anywhere, vmem],
        scratch_shapes=[pltpu.VMEM(shape, kind) for shape, kind in scratch]
        + [
            pltpu.SemaphoreType.DMA((chunks,)),
            pltpu.SemaphoreType.DMA((2,)),
            pltpu.SemaphoreType.DMA((3,)),
            pltpu.SemaphoreType.DMA((3,)),
            pltpu.SemaphoreType.DMA((16,)),
            pltpu.SemaphoreType.DMA((16,)),
            pltpu.SemaphoreType.DMA((3,)),
            pltpu.SemaphoreType.DMA,
        ],
        compiler_params=pltpu.CompilerParams(
            collective_id=0, has_side_effects=True, vmem_limit_bytes=64000 * 1024
        ),
    )(
        remap_src, kidx, owners * SLOTS + position, row_table, remap_src[None, :], atm_flux,
        land_sea, remap_weights, tracers, currents,
    )


def solution(mesh):
    tiles = P(None, None, ("sec", "gx"), "gy")
    shares = ("sec", "gx", "gy")

    def run(*args):
        return tuple(on_device(*args))

    return jax.shard_map(
        run,
        mesh=mesh,
        in_specs=(
            P(shares, None, None),
            P(shares, None, None),
            P(shares),
            P(shares),
            P(shares, None),
            tiles,
            tiles,
            P(("sec", "gx"), "gy"),
        ),
        out_specs=(tiles, P(shares, None)),
        check_vma=False,
    )
```

```python
import math

import jax
import jax.numpy as jnp
from jax import lax
from jax.experimental import pallas as pl
from jax.experimental.pallas import tpu as pltpu
from jax.sharding import PartitionSpec as P

KH = 0.1
KV = 0.1
CAP = 10
SLOTS = 16
KEPT = 5
TAIL = CAP - 8
ROWS = CAP * KEPT
LANES = 128
DEVICES = 128
CHUNK = 32
STRIP = 32
DECAY = math.exp(-0.25)
LOGICAL = pl.DeviceIdType.LOGICAL
MESH = pl.DeviceIdType.MESH
BF16 = jnp.bfloat16
F32 = jnp.float32
I32 = jnp.int32


class Torus:
    def __init__(self):
        sec, gx, gy = lax.axis_index("sec"), lax.axis_index("gx"), lax.axis_index("gy")
        self.band, self.gy = sec * 8 + gx, gy
        self.me = self.band * 8 + gy
        up, down = (self.band + 1) % 16, (self.band + 15) % 16
        self.north = (up // 8, up % 8, gy)
        self.south = (down // 8, down % 8, gy)
        self.east = (sec, gx, (gy + 1) % 8)
        self.west = (sec, gx, (gy + 7) % 8)
        self.y, self.z = (gy % 2) * 2 + sec, gx // 2
        self.xs = [((gy // 2 + d) % 4) * 2 for d in range(4)]
        self.cores = [((gx + d) % 2) * 8 for d in range(2)]

    def group(self, o):
        partners = []
        for d in (2, 1, 3, 0):
            y = (self.y + 3 - o % 4 + d) % 4
            z = (self.z + 3 - o // 4 + d) % 4
            base = (y % 2) * 64 + y // 2 + z * 16 + self.xs[d]
            partners += [base + self.cores[c] for c in (1, 0)]
        return partners

    def send_group(self, o, act):
        partners = self.group(o)
        for p in partners[:-1]:
            act(p)

        @pl.when(o < 15)
        def _():
            act(partners[-1])

    def each(self, act):
        def body(o, carry):
            self.send_group(o, act)
            return carry

        lax.fori_loop(0, 16, body, 0)


def wait_others(ref, sem, rows):
    first = pl.ds(0, DEVICES - 1)
    view = ref.at[first, pl.ds(0, rows)]
    pltpu.make_async_copy(view, view, sem).wait()


def coupled_kernel(
    src_ref, kidx_ref, slot_ref, row_ref, srcrow_ref, atm_ref, land_ref, w_hbm, q_hbm, uv_hbm,
    out_hbm, temp_ref,
    w_ref, part_ref, tmp_ref, send_ref, got_ref, srow_ref, rrow_ref, hot_ref, hott_ref, rest_ref,
    flux_ref, sret_ref, ret_ref, ret32_ref, terms_ref, srchot_ref,
    q_ref, uv_ref, q1_ref, q2_ref, coef_ref, open_ref, wet_ref,
    pe_ref, hx_ref, he_ref, hw_ref, pn_ref, ps_ref, hn_ref, hs_ref,
    heu_ref, hwu_ref, hnv_ref, hsv_ref,
    he1_ref, hw1_ref, hn1_ref, hs1_ref,
    pe2_ref, hx2_ref, he2_ref, hw2_ref, pn2_ref, ps2_ref, hn2_ref, hs2_ref,
    w_sem, in_sem, a2a_send, a2a_recv, side_send, side_recv, own_sem, out_sem,
):
    here = Torus()
    nonzeros = w_ref.shape[0]
    chunks = nonzeros // CHUNK
    levels = q_ref.shape[1]
    inner = pl.ds(8, LANES)

    def weight_copy(c):
        part = pl.ds(c * CHUNK, CHUNK)
        return pltpu.make_async_copy(w_hbm.at[part], w_ref.at[part], w_sem.at[c])

    def start_weights(c, carry):
        weight_copy(c).start()
        return carry

    q_copy = pltpu.make_async_copy(q_hbm, q_ref.at[:, :, inner], in_sem.at[0])
    uv_copy = pltpu.make_async_copy(uv_hbm, uv_ref.at[:, :, inner], in_sem.at[1])
    q_copy.start()
    uv_copy.start()
    lax.fori_loop(0, chunks, start_weights, 0)

    got_ref[...] = jnp.zeros_like(got_ref)
    barrier = pltpu.get_barrier_semaphore()
    here.each(
        lambda p: pl.semaphore_signal(barrier, inc=1, device_id=p, device_id_type=LOGICAL)
    )
    srow_ref[:, 0:1, :] = row_ref[...].reshape(DEVICES, 1, LANES)
    part_ref[nonzeros] = jnp.zeros((8, LANES), F32)
    pn_ref[...] = jnp.zeros_like(pn_ref)
    ps_ref[...] = jnp.zeros_like(ps_ref)
    pn2_ref[...] = jnp.zeros_like(pn2_ref)
    ps2_ref[...] = jnp.zeros_like(ps2_ref)

    sub = lax.broadcasted_iota(I32, (8, LANES), 0)
    takes = [
        jnp.where(sub < 2, 1.0, 0.0),
        jnp.where(sub == 1, 1.0, 0.0),
        jnp.where((sub == 1) | (sub == 2), 1.0, 0.0),
        jnp.where(sub == 2, -0.5, jnp.where((sub == 3) | (sub == 4), 1.0, 0.0)),
        jnp.where(sub == 1, -0.75, 0.0),
    ]
    blank = jnp.zeros((8, LANES), BF16)

    def combine(p):
        p = p.astype(BF16).astype(F32)
        total = p * takes[0]
        for up in range(1, 5):
            total = total + pltpu.roll(p, 8 - up, 0) * takes[up]
        return total

    def forward(c, carry):
        weight_copy(c).wait()
        for i in range(0, CHUNK, 2):
            k = c * CHUNK + i
            left = jnp.concatenate(
                [
                    jnp.concatenate([atm_ref[src_ref[k]], blank], axis=1),
                    jnp.concatenate([blank, atm_ref[src_ref[k + 1]]], axis=1),
                ],
                axis=0,
            )
            right = jnp.concatenate([w_ref[k], w_ref[k + 1]], axis=1)
            p = lax.dot_general(
                left, right, (((1,), (1,)), ((), ())), preferred_element_type=F32
            )
            part_ref[k] = combine(p[:8])
            part_ref[k + 1] = combine(p[8:])
        return carry

    def all_to_all(index, src, dst, cut):
        def act(p):
            pltpu.make_async_remote_copy(
                cut(src, p), cut(dst, here.me), a2a_send.at[index], a2a_recv.at[index],
                device_id=p, device_id_type=LOGICAL,
            ).start()

        return act

    class Ring:
        def __init__(self, index, east, west, north, south):
            self.index, self.pairs = index, (east, west, north, south)

        def start(self):
            targets = (here.east, here.west, here.north, here.south)
            for d, ((src, dst), target) in enumerate(zip(self.pairs, targets)):
                whole = pl.ds(0, src.shape[0])
                pltpu.make_async_remote_copy(
                    src.at[whole], dst.at[whole], side_send.at[self.index * 4 + d],
                    side_recv.at[self.index * 4 + d], device_id=target, device_id_type=MESH,
                ).start()

        def wait(self):
            for d, (src, dst) in enumerate(self.pairs):
                whole = pl.ds(0, src.shape[0])
                at = self.index * 4 + d
                pltpu.make_async_copy(src.at[whole], src.at[whole], side_send.at[at]).wait()
                pltpu.make_async_copy(dst.at[whole], dst.at[whole], side_recv.at[at]).wait()

    lane = lax.broadcasted_iota(I32, (LANES, LANES), 1)

    slane = lax.broadcasted_iota(I32, (STRIP, LANES), 1)
    pair = slane // 2
    strips = range(0, LANES, STRIP)

    def pack_columns(tiles, out_ref):
        for r in strips:
            packed = jnp.zeros((STRIP, LANES), F32)
            for i, tile in enumerate(tiles):
                packed = jnp.where(pair == i, pltpu.roll(tile(r), 2 * i + 1, 1), packed)
            out_ref[r : r + STRIP, :] = packed

    def join_columns(east_ref, west_ref, out_ref):
        for r in strips:
            at = slice(r, r + STRIP)
            out_ref[at, :] = jnp.where(
                slane % 2 == 0, pltpu.roll(east_ref[at, :], LANES - 1, 1),
                pltpu.roll(west_ref[at, :], 1, 1),
            )

    def strip_of(ref, *lead):
        return lambda r: ref[(*lead, slice(8 + r, 8 + r + STRIP), slice(None))]

    wet_ref[...] = jnp.zeros_like(wet_ref)
    wet_ref[inner, :] = land_ref[...].astype(F32)
    q_copy.wait()
    uv_copy.wait()

    jw = 3 * levels
    pack_columns(
        [strip_of(q_ref, t, l) for t in range(2) for l in range(levels)]
        + [strip_of(uv_ref, 0, l) for l in range(levels)]
        + [strip_of(wet_ref)],
        pe_ref,
    )
    for l in range(levels):
        for t in range(2):
            j = t * levels + l
            pn_ref[j : j + 1, :] = q_ref[t, l, LANES + 7 : LANES + 8, :]
            ps_ref[j : j + 1, :] = q_ref[t, l, 8:9, :]
        j = 2 * levels + l
        pn_ref[j : j + 1, :] = uv_ref[1, l, LANES + 7 : LANES + 8, :]
        ps_ref[j : j + 1, :] = uv_ref[1, l, 8:9, :]
    pn_ref[jw : jw + 1, :] = wet_ref[LANES + 7 : LANES + 8, :]
    ps_ref[jw : jw + 1, :] = wet_ref[8:9, :]
    inputs_ring = Ring(
        0, (pe_ref, hw_ref), (pe_ref, he_ref), (pn_ref, hs_ref), (ps_ref, hn_ref)
    )

    lax.fori_loop(0, chunks // 2, forward, 0)
    pl.semaphore_wait(barrier, DEVICES - 1)
    here.each(all_to_all(0, srow_ref, rrow_ref, lambda ref, i: ref.at[i, pl.ds(0, 1)]))
    inputs_ring.start()
    lax.fori_loop(chunks // 2, chunks, forward, 0)
    send_flux = all_to_all(1, send_ref, got_ref, lambda ref, i: ref.at[i, pl.ds(0, ROWS)])

    def pack(o, carry):
        partners = here.group(o)
        for i, p in enumerate(partners):
            found = [part_ref[kidx_ref[p * CAP + s]] for s in range(CAP)]
            for s in range(8):
                tmp_ref[i, s * 8 : s * 8 + 8, :] = found[s]
            shifted = pltpu.roll(found[9], KEPT, 0)
            send_ref[p, 40:48] = jnp.where(sub < KEPT, found[8], shifted).astype(BF16)
            send_ref[p, 48:56] = shifted.astype(BF16)
        for i, p in enumerate(partners):
            for f in range(KEPT):
                send_ref[p, f * 8 : f * 8 + 8] = tmp_ref[
                    i, pl.ds(f, 8, stride=8), :
                ].astype(BF16)

        @pl.when(o > 0)
        def _():
            here.send_group(o - 1, send_flux)

        return carry

    lax.fori_loop(0, 16, pack, 0)
    own_rows = pltpu.make_async_copy(
        srow_ref.at[here.me, pl.ds(0, 1)], rrow_ref.at[here.me, pl.ds(0, 1)], own_sem.at[0]
    )
    own_rows.start()
    here.send_group(15, send_flux)
    own_flux = pltpu.make_async_copy(send_ref.at[here.me], got_ref.at[here.me], own_sem.at[1])
    own_flux.start()

    own_rows.wait()
    wait_others(srow_ref, a2a_send.at[0], 1)
    wait_others(rrow_ref, a2a_recv.at[0], 1)
    rows = rrow_ref[:, 0:1, :].reshape(DEVICES, LANES).astype(BF16)
    upright = lax.broadcasted_iota(I32, (LANES, LANES), 0)
    ones = jnp.ones((LANES, LANES), BF16)

    def spread_rows(b, each):
        pick = (lane == b * (LANES // each) + upright // each).astype(F32).astype(BF16)
        spread = jnp.dot(pick, rows, preferred_element_type=F32)
        return jnp.where(lane == upright % each, spread, 0.0).astype(BF16)

    for b in range(SLOTS):
        down = jnp.dot(spread_rows(b, SLOTS), ones, preferred_element_type=F32)
        hott_ref[b * LANES : (b + 1) * LANES, :] = (
            (down == lane.astype(F32)).astype(F32).astype(BF16)
        )
    for b in range(8):
        across = lax.dot_general(
            ones, spread_rows(b, 8), (((1,), (1,)), ((), ())), preferred_element_type=F32
        )
        hot_ref[:, b * LANES : (b + 1) * LANES] = (
            (across == upright.astype(F32)).astype(F32).astype(BF16)
        )
    turned = jnp.transpose(rrow_ref[:, 0:1, :].reshape(DEVICES, LANES))
    for i in range(TAIL):
        hot_ref[:, (8 + i) * LANES : (9 + i) * LANES] = (
            (turned[8 + i : 9 + i, :] == upright.astype(F32)).astype(F32).astype(BF16)
        )
    blocks = temp_ref.shape[0]
    block = lax.broadcasted_iota(I32, (blocks, LANES), 0)
    for i in range(nonzeros // LANES):
        srchot_ref[:, i * LANES : (i + 1) * LANES] = (
            (block == srcrow_ref[i : i + 1, :]).astype(F32).astype(BF16)
        )

    inputs_ring.wait()
    inside_e = jnp.where(here.gy < 7, 1.0, 0.0)
    inside_w = jnp.where(here.gy > 0, 1.0, 0.0)
    inside_n = jnp.where(here.band < 15, 1.0, 0.0)
    inside_s = jnp.where(here.band > 0, 1.0, 0.0)
    wet_ref[LANES + 8 : LANES + 9, :] = hn_ref[jw : jw + 1, :] * inside_n
    wet_ref[7:8, :] = hs_ref[jw : jw + 1, :] * inside_s
    join_columns(he_ref, hw_ref, hx_ref)

    def columns_by(ref, r, i):
        return pltpu.roll(ref[r : r + STRIP, :], LANES - 1 - 2 * i, 1)

    def east_west(tile, both):
        return (
            jnp.where(slane == LANES - 1, both, pltpu.roll(tile, LANES - 1, 1)),
            jnp.where(slane == 0, both, pltpu.roll(tile, 1, 1)),
        )

    for r in strips:
        wet = wet_ref[8 + r : 8 + r + STRIP, :]
        both = columns_by(hx_ref, r, jw)
        east, west = east_west(wet, jnp.where(slane == 0, both * inside_w, both * inside_e))
        open_ref[0, r : r + STRIP, :] = wet * east
        open_ref[1, r : r + STRIP, :] = wet * west
        open_ref[2, r : r + STRIP, :] = wet * wet_ref[9 + r : 9 + r + STRIP, :]
        open_ref[3, r : r + STRIP, :] = wet * wet_ref[7 + r : 7 + r + STRIP, :]

    def coefficients(l):
        j = 2 * levels + l
        uv_ref[1, l, LANES + 8 : LANES + 9, :] = hn_ref[pl.ds(j, 1), :]
        uv_ref[1, l, 7:8, :] = hs_ref[pl.ds(j, 1), :]
        for r in strips:
            at = slice(r, r + STRIP)
            u = uv_ref[0, l, 8 + r : 8 + r + STRIP, :]
            east, west = east_west(u, columns_by(hx_ref, r, j))
            v = uv_ref[1, l, 8 + r : 8 + r + STRIP, :]
            north = uv_ref[1, l, 9 + r : 9 + r + STRIP, :]
            south = uv_ref[1, l, 7 + r : 7 + r + STRIP, :]
            loss = 1.0 - 2.0 * KV * wet_ref[8 + r : 8 + r + STRIP, :]
            for d, (sign, beside, own) in enumerate(
                ((-1.0, east, u), (1.0, west, u), (-1.0, north, v), (1.0, south, v))
            ):
                gate = open_ref[d, at, :]
                flow = (0.25 * sign) * (own + beside) * gate
                coef_ref[d, l, at, :] = KH * gate + flow
                loss = loss - (KH * gate - flow)
            coef_ref[4, l, at, :] = loss

    def advance(ref, t, l, r, both):
        at = slice(r, r + STRIP)
        mid = slice(8 + r, 8 + r + STRIP)
        c = ref[t, l, mid, :]
        east, west = east_west(c, both)
        fixed = isinstance(l, int)
        above = c if fixed and l == 0 else ref[t, l - 1, mid, :]
        below = c if fixed and l == levels - 1 else ref[t, l + 1, mid, :]
        return (
            coef_ref[4, l, at, :] * c
            + coef_ref[0, l, at, :] * east
            + coef_ref[1, l, at, :] * west
            + coef_ref[2, l, at, :] * ref[t, l, 9 + r : 9 + r + STRIP, :]
            + coef_ref[3, l, at, :] * ref[t, l, 7 + r : 7 + r + STRIP, :]
            + (KV * wet_ref[mid, :]) * (above + below)
        )

    def set_rows(ref, t, l, north, south):
        ref[t, l, LANES + 8 : LANES + 9, :] = north
        ref[t, l, 7:8, :] = south

    def first_step(l, carry):
        coefficients(l)
        for t in range(2):
            j = t * levels + l
            set_rows(q_ref, t, l, hn_ref[pl.ds(j, 1), :], hs_ref[pl.ds(j, 1), :])
            for r in strips:
                q1_ref[t, l, 8 + r : 8 + r + STRIP, :] = advance(
                    q_ref, t, l, r, columns_by(hx_ref, r, j)
                )
        return carry

    lax.fori_loop(1, levels - 1, first_step, 0)
    first_step(levels - 1, 0)

    own_flux.wait()
    wait_others(got_ref, a2a_recv.at[1], ROWS)
    rest_ref[...] = got_ref[:, 40:56, :].astype(F32).reshape(DEVICES * SLOTS, LANES)

    def field(f):
        body = got_ref[:, f * 8 : f * 8 + 8, :].astype(F32).reshape(DEVICES * 8, LANES)
        tails = [
            rest_ref[pl.ds(i * KEPT + f, DEVICES, stride=SLOTS), :] for i in range(TAIL)
        ]
        return jnp.concatenate([body] + tails, axis=0).astype(BF16)

    for f in range(0, KEPT, 2):
        fields = [field(g) for g in range(f, min(f + 2, KEPT))]
        total = jnp.dot(
            hot_ref[...], jnp.concatenate(fields, axis=1), preferred_element_type=F32
        )
        for i in range(len(fields)):
            flux_ref[f + i] = total[:, i * LANES : (i + 1) * LANES]
    flux_ring = Ring(
        1, (flux_ref.at[3], hwu_ref), (flux_ref.at[3], heu_ref),
        (flux_ref.at[4, pl.ds(LANES - 8, 8)], hsv_ref), (flux_ref.at[4, pl.ds(0, 8)], hnv_ref),
    )
    flux_ring.start()
    wait_others(send_ref, a2a_send.at[1], ROWS)
    heat_scale = 0.3 * (1.0 - DECAY)

    def warmed(t, l, r, scale):
        at, mid = slice(r, r + STRIP), slice(8 + r, 8 + r + STRIP)
        q1_ref[t, l, mid, :] = q1_ref[t, l, mid, :] + wet_ref[mid, :] * (
            scale * flux_ref[0, at, :]
        )

    for r in strips:
        at, mid = slice(r, r + STRIP), slice(8 + r, 8 + r + STRIP)
        uv_ref[0, 0, mid, :] = uv_ref[0, 0, mid, :] + 0.1 * flux_ref[3, at, :]
        uv_ref[1, 0, mid, :] = uv_ref[1, 0, mid, :] + 0.1 * flux_ref[4, at, :]
        warmed(0, 1, r, heat_scale * DECAY)
    for t in range(2):
        j = t * levels
        set_rows(q_ref, t, 0, hn_ref[j : j + 1, :], hs_ref[j : j + 1, :])
    flux_ring.wait()
    ju = 2 * levels
    hx_ref[...] = hx_ref[...] + 0.1 * jnp.where(
        lane == 2 * ju, pltpu.roll(heu_ref[...], 2 * ju, 1),
        jnp.where(lane == 2 * ju + 1, pltpu.roll(hwu_ref[...], 2 * ju + 2, 1), 0.0),
    )
    hn_ref[ju : ju + 1, :] = hn_ref[ju : ju + 1, :] + 0.1 * hnv_ref[0:1, :]
    hs_ref[ju : ju + 1, :] = hs_ref[ju : ju + 1, :] + 0.1 * hsv_ref[7:8, :]
    coefficients(0)

    def surface(t, r):
        at = slice(r, r + STRIP)
        if t == 0:
            force = heat_scale * flux_ref[0, at, :] + 0.2 * flux_ref[1, at, :]
        else:
            force = 0.2 * flux_ref[2, at, :]
        return wet_ref[8 + r : 8 + r + STRIP, :] * force

    def surface_step(t):
        j = t * levels
        for r in strips:
            q1_ref[t, 0, 8 + r : 8 + r + STRIP, :] = advance(
                q_ref, t, 0, r, columns_by(hx_ref, r, j)
            ) + surface(t, r)

    surface_step(0)
    top_ring = Ring(
        2, (q1_ref.at[0, 0, inner], hw1_ref), (q1_ref.at[0, 0, inner], he1_ref),
        (q1_ref.at[0, 0, pl.ds(LANES, 8)], hs1_ref), (q1_ref.at[0, 0, pl.ds(8, 8)], hn1_ref),
    )
    top_ring.start()
    surface_step(1)

    def forced(l, scale):
        for r in strips:
            warmed(0, l, r, scale)
        return scale * DECAY

    lax.fori_loop(2, levels, forced, jnp.float32(heat_scale * DECAY * DECAY))

    pack_columns([strip_of(q1_ref, t, l) for t in range(2) for l in range(levels)], pe2_ref)
    for l in range(levels):
        for t in range(2):
            j = t * levels + l
            pn2_ref[j : j + 1, :] = q1_ref[t, l, LANES + 7 : LANES + 8, :]
            ps2_ref[j : j + 1, :] = q1_ref[t, l, 8:9, :]
    last_ring = Ring(
        3, (pe2_ref, hw2_ref), (pe2_ref, he2_ref), (pn2_ref, hs2_ref), (ps2_ref, hn2_ref)
    )
    last_ring.start()
    top_ring.wait()
    set_rows(q1_ref, 0, 0, hn1_ref[0:1, :], hs1_ref[7:8, :])
    for r in strips:
        q2_ref[0, 0, r : r + STRIP, :] = advance(
            q1_ref, 0, 0, r,
            jnp.where(
                slane == 0, pltpu.roll(hw1_ref[r : r + STRIP, :], 1, 1),
                pltpu.roll(he1_ref[r : r + STRIP, :], LANES - 1, 1),
            ),
        ) + surface(0, r)

    sst = q2_ref[0, 0].astype(BF16)

    def select(b, carry):
        at = pl.ds(pl.multiple_of(b * LANES, LANES), LANES)
        picked = jnp.dot(hott_ref[at, :], sst, preferred_element_type=F32).astype(BF16)
        sret_ref[pl.ds(b * 8, 8)] = picked.reshape(8, SLOTS, LANES)
        return carry

    lax.fori_loop(0, SLOTS, select, 0)
    here.each(all_to_all(2, sret_ref, ret_ref, lambda ref, i: ref.at[i, pl.ds(0, CAP)]))
    own_ret = pltpu.make_async_copy(sret_ref.at[here.me], ret_ref.at[here.me], own_sem.at[2])
    own_ret.start()

    last_ring.wait()
    join_columns(he2_ref, hw2_ref, hx2_ref)

    def second(t, l, r):
        j = t * levels + l
        return advance(q1_ref, t, l, r, columns_by(hx2_ref, r, j))

    def rows_of(t, l):
        j = t * levels + l
        set_rows(q1_ref, t, l, hn2_ref[pl.ds(j, 1), :], hs2_ref[pl.ds(j, 1), :])

    rows_of(1, 0)
    for r in strips:
        q2_ref[1, 0, r : r + STRIP, :] = second(1, 0, r) + surface(1, r)

    def second_step(l, scale):
        for t in range(2):
            rows_of(t, l)
            for r in strips:
                fresh = second(t, l, r)
                if t == 0:
                    fresh = fresh + wet_ref[8 + r : 8 + r + STRIP, :] * (
                        scale * flux_ref[0, r : r + STRIP, :]
                    )
                q2_ref[t, l, r : r + STRIP, :] = fresh
        return scale * DECAY

    scale = lax.fori_loop(1, levels - 1, second_step, jnp.float32(heat_scale * DECAY))
    second_step(levels - 1, scale)
    out_copy = pltpu.make_async_copy(q2_ref, out_hbm, out_sem)
    out_copy.start()

    own_ret.wait()
    wait_others(sret_ref, a2a_send.at[2], CAP)
    wait_others(ret_ref, a2a_recv.at[2], CAP)
    ret32_ref[pl.ds(0, DEVICES * SLOTS), :] = ret_ref[...].astype(F32).reshape(DEVICES * SLOTS, LANES)

    def backward(c, carry):
        for g in range(0, CHUNK, 8):
            base = c * CHUNK + g
            picked = jnp.concatenate(
                [ret32_ref[pl.ds(slot_ref[base + i], 1), :] for i in range(8)], axis=0
            )
            left = jnp.concatenate(
                [jnp.where(sub == i, picked, 0.0).astype(BF16) for i in range(8)], axis=1
            )
            right = w_ref[pl.ds(base, 8)].reshape(8 * LANES, LANES)
            terms_ref[pl.ds(pl.multiple_of(base, 8), 8), :] = jnp.dot(
                left, right, preferred_element_type=F32
            )
        return carry

    lax.fori_loop(0, chunks, backward, 0)
    terms = terms_ref[...]
    high = terms.astype(BF16)
    low = (terms - high.astype(F32)).astype(BF16)
    temp_ref[...] = jnp.dot(srchot_ref[...], high, preferred_element_type=F32) + jnp.dot(
        srchot_ref[...], low, preferred_element_type=F32
    )
    out_copy.wait()


def on_device(
    atm_flux, remap_weights, remap_src, remap_dst, remap_owner, tracers, currents, land_sea
):
    nonzeros, width = remap_weights.shape[0], remap_weights.shape[1]
    atm_blocks = atm_flux.shape[0]
    levels = tracers.shape[1]
    chunks = nonzeros // CHUNK

    owners = remap_owner[:, 0]
    hot = (owners[:, None] == jnp.arange(DEVICES, dtype=I32)[None, :]).astype(BF16)
    order = jnp.arange(nonzeros, dtype=I32)
    before = (order[:, None] > order[None, :]).astype(BF16)
    earlier = jnp.dot(before, hot, preferred_element_type=F32)
    position = jnp.sum(earlier * hot.astype(F32), axis=1).astype(I32)
    slot = owners * CAP + position
    taken = jnp.arange(DEVICES * CAP, dtype=I32)[:, None] == slot[None, :]
    kidx = jnp.sum(jnp.where(taken, order[None, :] - nonzeros, 0), axis=1) + nonzeros
    slot_rows = jnp.sum(jnp.where(taken, remap_dst[None, :] - 200, 0), axis=1) + 200
    row_table = jnp.pad(
        slot_rows.reshape(DEVICES, CAP).astype(F32), ((0, 0), (0, LANES - CAP)),
        constant_values=200.0,
    )

    vmem = pl.BlockSpec(memory_space=pltpu.VMEM)
    smem = pl.BlockSpec(memory_space=pltpu.SMEM)
    anywhere = pl.BlockSpec(memory_space=pl.ANY)
    padded = (2, levels, LANES + 16, LANES)
    tile = (LANES, LANES)
    scratch = [
        (remap_weights.shape, BF16), ((nonzeros + 1, 8, LANES), F32), ((8, 64, LANES), F32),
        ((DEVICES, 56, width), BF16), ((DEVICES, 56, width), BF16),
        ((DEVICES, 8, LANES), F32), ((DEVICES, 8, LANES), F32),
        ((LANES, DEVICES * CAP), BF16), ((DEVICES * SLOTS, LANES), BF16), ((DEVICES * SLOTS, LANES), F32),
        ((KEPT,) + tile, F32),
        ((DEVICES, SLOTS, width), BF16), ((DEVICES, SLOTS, width), BF16),
        ((DEVICES * SLOTS + 8, width), F32), ((nonzeros, width), F32), ((atm_blocks, nonzeros), BF16),
        (padded, F32), (padded, F32), (padded, F32), (tracers.shape, F32),
        ((5, levels) + tile, F32), ((4,) + tile, F32), ((LANES + 16, LANES), F32),
        (tile, F32), (tile, F32), (tile, F32), (tile, F32),
        (tile, F32), (tile, F32), (tile, F32), (tile, F32),
        (tile, F32), (tile, F32), ((8, LANES), F32), ((8, LANES), F32),
        (tile, F32), (tile, F32), ((8, LANES), F32), ((8, LANES), F32),
        (tile, F32), (tile, F32), (tile, F32), (tile, F32),
        (tile, F32), (tile, F32), (tile, F32), (tile, F32),
    ]
    return pl.pallas_call(
        coupled_kernel,
        name="coupled",
        out_shape=[
            jax.ShapeDtypeStruct(tracers.shape, F32),
            jax.ShapeDtypeStruct((atm_blocks, width), F32),
        ],
        in_specs=[smem, smem, smem, vmem, vmem, vmem, vmem, anywhere, anywhere, anywhere],
        out_specs=[anywhere, vmem],
        scratch_shapes=[pltpu.VMEM(shape, kind) for shape, kind in scratch]
        + [
            pltpu.SemaphoreType.DMA((chunks,)),
            pltpu.SemaphoreType.DMA((2,)),
            pltpu.SemaphoreType.DMA((3,)),
            pltpu.SemaphoreType.DMA((3,)),
            pltpu.SemaphoreType.DMA((16,)),
            pltpu.SemaphoreType.DMA((16,)),
            pltpu.SemaphoreType.DMA((3,)),
            pltpu.SemaphoreType.DMA,
        ],
        compiler_params=pltpu.CompilerParams(
            collective_id=0, has_side_effects=True, vmem_limit_bytes=64000 * 1024
        ),
    )(
        remap_src, kidx, owners * SLOTS + position, row_table, remap_src.reshape(nonzeros // LANES, LANES), atm_flux,
        land_sea, remap_weights, tracers, currents,
    )


def solution(mesh):
    tiles = P(None, None, ("sec", "gx"), "gy")
    shares = ("sec", "gx", "gy")

    def run(*args):
        return tuple(on_device(*args))

    return jax.shard_map(
        run,
        mesh=mesh,
        in_specs=(
            P(shares, None, None),
            P(shares, None, None),
            P(shares),
            P(shares),
            P(shares, None),
            tiles,
            tiles,
            P(("sec", "gx"), "gy"),
        ),
        out_specs=(tiles, P(shares, None)),
        check_vma=False,
    )
```

```python
import math

import jax
import jax.numpy as jnp
from jax import lax
from jax.experimental import pallas as pl
from jax.experimental.pallas import tpu as pltpu
from jax.sharding import PartitionSpec as P

KH = 0.1
KV = 0.1
CAP = 10
SLOTS = 16
KEPT = 5
TAIL = CAP - 8
ROWS = CAP * KEPT
LANES = 128
DEVICES = 128
CHUNK = 32
STRIP = 32
DECAY = math.exp(-0.25)
LOGICAL = pl.DeviceIdType.LOGICAL
MESH = pl.DeviceIdType.MESH
BF16 = jnp.bfloat16
F32 = jnp.float32
I32 = jnp.int32


class Torus:
    def __init__(self):
        sec, gx, gy = lax.axis_index("sec"), lax.axis_index("gx"), lax.axis_index("gy")
        self.band, self.gy = sec * 8 + gx, gy
        self.me = self.band * 8 + gy
        up, down = (self.band + 1) % 16, (self.band + 15) % 16
        self.north = (up // 8, up % 8, gy)
        self.south = (down // 8, down % 8, gy)
        self.east = (sec, gx, (gy + 1) % 8)
        self.west = (sec, gx, (gy + 7) % 8)
        self.y, self.z = (gy % 2) * 2 + sec, gx // 2
        self.xs = [((gy // 2 + d) % 4) * 2 for d in range(4)]
        self.cores = [((gx + d) % 2) * 8 for d in range(2)]

    def group(self, o):
        partners = []
        for d in (2, 1, 3, 0):
            y = (self.y + 3 - o % 4 + d) % 4
            z = (self.z + 3 - o // 4 + d) % 4
            base = (y % 2) * 64 + y // 2 + z * 16 + self.xs[d]
            partners += [base + self.cores[c] for c in (1, 0)]
        return partners

    def send_group(self, o, act):
        partners = self.group(o)
        for p in partners[:-1]:
            act(p)

        @pl.when(o < 15)
        def _():
            act(partners[-1])

    def each(self, act):
        def body(o, carry):
            self.send_group(o, act)
            return carry

        lax.fori_loop(0, 16, body, 0)


def wait_others(ref, sem, rows):
    first = pl.ds(0, DEVICES - 1)
    view = ref.at[first, pl.ds(0, rows)]
    pltpu.make_async_copy(view, view, sem).wait()


def coupled_kernel(
    src_ref, kidx_ref, slot_ref, row_ref, srcrow_ref, atm_ref, land_ref, w_hbm, q_hbm, uv_hbm,
    out_hbm, temp_ref,
    w_ref, part_ref, tmp_ref, send_ref, got_ref, srow_ref, rrow_ref, hot_ref, hott_ref, rest_ref,
    flux_ref, sret_ref, ret_ref, ret32_ref, terms_ref, srchot_ref,
    q_ref, uv_ref, q1_ref, q2_ref, coef_ref, open_ref, wet_ref,
    pe_ref, hx_ref, he_ref, hw_ref, pn_ref, ps_ref, hn_ref, hs_ref,
    heu_ref, hwu_ref, hnv_ref, hsv_ref,
    he1_ref, hw1_ref, hn1_ref, hs1_ref,
    pe2_ref, hx2_ref, he2_ref, hw2_ref, pn2_ref, ps2_ref, hn2_ref, hs2_ref,
    w_sem, in_sem, a2a_send, a2a_recv, side_send, side_recv, own_sem, out_sem,
):
    here = Torus()
    nonzeros = w_ref.shape[0]
    chunks = nonzeros // CHUNK
    levels = q_ref.shape[1]
    inner = pl.ds(8, LANES)

    def weight_copy(c):
        part = pl.ds(c * CHUNK, CHUNK)
        return pltpu.make_async_copy(w_hbm.at[part], w_ref.at[part], w_sem.at[c])

    def start_weights(c, carry):
        weight_copy(c).start()
        return carry

    q_copy = pltpu.make_async_copy(q_hbm, q_ref.at[:, :, inner], in_sem.at[0])
    uv_copy = pltpu.make_async_copy(uv_hbm, uv_ref.at[:, :, inner], in_sem.at[1])
    q_copy.start()
    uv_copy.start()
    lax.fori_loop(0, chunks, start_weights, 0)

    got_ref[...] = jnp.zeros_like(got_ref)
    barrier = pltpu.get_barrier_semaphore()
    here.each(
        lambda p: pl.semaphore_signal(barrier, inc=1, device_id=p, device_id_type=LOGICAL)
    )
    srow_ref[:, 0:1, :] = row_ref[...].reshape(DEVICES, 1, LANES)
    part_ref[nonzeros] = jnp.zeros((8, LANES), F32)
    pn_ref[...] = jnp.zeros_like(pn_ref)
    ps_ref[...] = jnp.zeros_like(ps_ref)
    pn2_ref[...] = jnp.zeros_like(pn2_ref)
    ps2_ref[...] = jnp.zeros_like(ps2_ref)

    sub = lax.broadcasted_iota(I32, (8, LANES), 0)
    takes = [
        jnp.where(sub < 2, 1.0, 0.0),
        jnp.where(sub == 1, 1.0, 0.0),
        jnp.where((sub == 1) | (sub == 2), 1.0, 0.0),
        jnp.where(sub == 2, -0.5, jnp.where((sub == 3) | (sub == 4), 1.0, 0.0)),
        jnp.where(sub == 1, -0.75, 0.0),
    ]
    blank = jnp.zeros((8, LANES), BF16)

    def combine(p):
        p = p.astype(BF16).astype(F32)
        total = p * takes[0]
        for up in range(1, 5):
            total = total + pltpu.roll(p, 8 - up, 0) * takes[up]
        return total

    def forward(c, carry):
        weight_copy(c).wait()
        for i in range(0, CHUNK, 2):
            k = c * CHUNK + i
            left = jnp.concatenate(
                [
                    jnp.concatenate([atm_ref[src_ref[k]], blank], axis=1),
                    jnp.concatenate([blank, atm_ref[src_ref[k + 1]]], axis=1),
                ],
                axis=0,
            )
            right = jnp.concatenate([w_ref[k], w_ref[k + 1]], axis=1)
            p = lax.dot_general(
                left, right, (((1,), (1,)), ((), ())), preferred_element_type=F32
            )
            part_ref[k] = combine(p[:8])
            part_ref[k + 1] = combine(p[8:])
        return carry

    def all_to_all(index, src, dst, cut):
        def act(p):
            pltpu.make_async_remote_copy(
                cut(src, p), cut(dst, here.me), a2a_send.at[index], a2a_recv.at[index],
                device_id=p, device_id_type=LOGICAL,
            ).start()

        return act

    class Ring:
        def __init__(self, index, east, west, north, south):
            self.index, self.pairs = index, (east, west, north, south)

        def start(self):
            targets = (here.east, here.west, here.north, here.south)
            for d, ((src, dst), target) in enumerate(zip(self.pairs, targets)):
                whole = pl.ds(0, src.shape[0])
                pltpu.make_async_remote_copy(
                    src.at[whole], dst.at[whole], side_send.at[self.index * 4 + d],
                    side_recv.at[self.index * 4 + d], device_id=target, device_id_type=MESH,
                ).start()

        def wait(self):
            for d, (src, dst) in enumerate(self.pairs):
                whole = pl.ds(0, src.shape[0])
                at = self.index * 4 + d
                pltpu.make_async_copy(src.at[whole], src.at[whole], side_send.at[at]).wait()
                pltpu.make_async_copy(dst.at[whole], dst.at[whole], side_recv.at[at]).wait()

    lane = lax.broadcasted_iota(I32, (LANES, LANES), 1)

    slane = lax.broadcasted_iota(I32, (STRIP, LANES), 1)
    pair = slane // 2
    strips = range(0, LANES, STRIP)

    def pack_columns(tiles, out_ref):
        for r in strips:
            packed = jnp.zeros((STRIP, LANES), F32)
            for i, tile in enumerate(tiles):
                packed = jnp.where(pair == i, pltpu.roll(tile(r), 2 * i + 1, 1), packed)
            out_ref[r : r + STRIP, :] = packed

    def join_columns(east_ref, west_ref, out_ref):
        for r in strips:
            at = slice(r, r + STRIP)
            out_ref[at, :] = jnp.where(
                slane % 2 == 0, pltpu.roll(east_ref[at, :], LANES - 1, 1),
                pltpu.roll(west_ref[at, :], 1, 1),
            )

    def strip_of(ref, *lead):
        return lambda r: ref[(*lead, slice(8 + r, 8 + r + STRIP), slice(None))]

    wet_ref[...] = jnp.zeros_like(wet_ref)
    wet_ref[inner, :] = land_ref[...].astype(F32)
    q_copy.wait()
    uv_copy.wait()

    jw = 3 * levels
    pack_columns(
        [strip_of(q_ref, t, l) for t in range(2) for l in range(levels)]
        + [strip_of(uv_ref, 0, l) for l in range(levels)]
        + [strip_of(wet_ref)],
        pe_ref,
    )
    for l in range(levels):
        for t in range(2):
            j = t * levels + l
            pn_ref[j : j + 1, :] = q_ref[t, l, LANES + 7 : LANES + 8, :]
            ps_ref[j : j + 1, :] = q_ref[t, l, 8:9, :]
        j = 2 * levels + l
        pn_ref[j : j + 1, :] = uv_ref[1, l, LANES + 7 : LANES + 8, :]
        ps_ref[j : j + 1, :] = uv_ref[1, l, 8:9, :]
    pn_ref[jw : jw + 1, :] = wet_ref[LANES + 7 : LANES + 8, :]
    ps_ref[jw : jw + 1, :] = wet_ref[8:9, :]
    inputs_ring = Ring(
        0, (pe_ref, hw_ref), (pe_ref, he_ref), (pn_ref, hs_ref), (ps_ref, hn_ref)
    )

    lax.fori_loop(0, chunks // 2, forward, 0)
    pl.semaphore_wait(barrier, DEVICES - 1)
    here.each(all_to_all(0, srow_ref, rrow_ref, lambda ref, i: ref.at[i, pl.ds(0, 1)]))
    inputs_ring.start()
    lax.fori_loop(chunks // 2, chunks, forward, 0)
    send_flux = all_to_all(1, send_ref, got_ref, lambda ref, i: ref.at[i, pl.ds(0, ROWS)])

    def pack(o, carry):
        partners = here.group(o)
        for i, p in enumerate(partners):
            found = [part_ref[kidx_ref[p * CAP + s]] for s in range(CAP)]
            for s in range(8):
                tmp_ref[i, s * 8 : s * 8 + 8, :] = found[s]
            shifted = pltpu.roll(found[9], KEPT, 0)
            send_ref[p, 40:48] = jnp.where(sub < KEPT, found[8], shifted).astype(BF16)
            send_ref[p, 48:56] = shifted.astype(BF16)
        for i, p in enumerate(partners):
            for f in range(KEPT):
                send_ref[p, f * 8 : f * 8 + 8] = tmp_ref[
                    i, pl.ds(f, 8, stride=8), :
                ].astype(BF16)

        @pl.when(o > 0)
        def _():
            here.send_group(o - 1, send_flux)

        return carry

    lax.fori_loop(0, 16, pack, 0)
    own_rows = pltpu.make_async_copy(
        srow_ref.at[here.me, pl.ds(0, 1)], rrow_ref.at[here.me, pl.ds(0, 1)], own_sem.at[0]
    )
    own_rows.start()
    here.send_group(15, send_flux)
    own_flux = pltpu.make_async_copy(send_ref.at[here.me], got_ref.at[here.me], own_sem.at[1])
    own_flux.start()

    own_rows.wait()
    wait_others(srow_ref, a2a_send.at[0], 1)
    wait_others(rrow_ref, a2a_recv.at[0], 1)
    rows = rrow_ref[:, 0:1, :].reshape(DEVICES, LANES).astype(BF16)
    upright = lax.broadcasted_iota(I32, (LANES, LANES), 0)
    ones = jnp.ones((LANES, LANES), BF16)

    def spread_rows(b, each):
        pick = (lane == b * (LANES // each) + upright // each).astype(F32).astype(BF16)
        spread = jnp.dot(pick, rows, preferred_element_type=F32)
        return jnp.where(lane == upright % each, spread, 0.0).astype(BF16)

    for b in range(SLOTS):
        down = jnp.dot(spread_rows(b, SLOTS), ones, preferred_element_type=F32)
        hott_ref[b * LANES : (b + 1) * LANES, :] = (
            (down == lane.astype(F32)).astype(F32).astype(BF16)
        )
    for b in range(8):
        across = lax.dot_general(
            ones, spread_rows(b, 8), (((1,), (1,)), ((), ())), preferred_element_type=F32
        )
        hot_ref[:, b * LANES : (b + 1) * LANES] = (
            (across == upright.astype(F32)).astype(F32).astype(BF16)
        )
    turned = jnp.transpose(rrow_ref[:, 0:1, :].reshape(DEVICES, LANES))
    for i in range(TAIL):
        hot_ref[:, (8 + i) * LANES : (9 + i) * LANES] = (
            (turned[8 + i : 9 + i, :] == upright.astype(F32)).astype(F32).astype(BF16)
        )
    blocks = temp_ref.shape[0]
    block = lax.broadcasted_iota(I32, (blocks, LANES), 0)
    for i in range(nonzeros // LANES):
        srchot_ref[:, i * LANES : (i + 1) * LANES] = (
            (block == srcrow_ref[i : i + 1, :]).astype(F32).astype(BF16)
        )

    inputs_ring.wait()
    inside_e = jnp.where(here.gy < 7, 1.0, 0.0)
    inside_w = jnp.where(here.gy > 0, 1.0, 0.0)
    inside_n = jnp.where(here.band < 15, 1.0, 0.0)
    inside_s = jnp.where(here.band > 0, 1.0, 0.0)
    wet_ref[LANES + 8 : LANES + 9, :] = hn_ref[jw : jw + 1, :] * inside_n
    wet_ref[7:8, :] = hs_ref[jw : jw + 1, :] * inside_s
    join_columns(he_ref, hw_ref, hx_ref)

    def columns_by(ref, r, i):
        return pltpu.roll(ref[r : r + STRIP, :], LANES - 1 - 2 * i, 1)

    def east_west(tile, both):
        return (
            jnp.where(slane == LANES - 1, both, pltpu.roll(tile, LANES - 1, 1)),
            jnp.where(slane == 0, both, pltpu.roll(tile, 1, 1)),
        )

    for r in strips:
        wet = wet_ref[8 + r : 8 + r + STRIP, :]
        both = columns_by(hx_ref, r, jw)
        east, west = east_west(wet, jnp.where(slane == 0, both * inside_w, both * inside_e))
        open_ref[0, r : r + STRIP, :] = wet * east
        open_ref[1, r : r + STRIP, :] = wet * west
        open_ref[2, r : r + STRIP, :] = wet * wet_ref[9 + r : 9 + r + STRIP, :]
        open_ref[3, r : r + STRIP, :] = wet * wet_ref[7 + r : 7 + r + STRIP, :]

    def coefficients(l):
        j = 2 * levels + l
        uv_ref[1, l, LANES + 8 : LANES + 9, :] = hn_ref[pl.ds(j, 1), :]
        uv_ref[1, l, 7:8, :] = hs_ref[pl.ds(j, 1), :]
        for r in strips:
            at = slice(r, r + STRIP)
            u = uv_ref[0, l, 8 + r : 8 + r + STRIP, :]
            east, west = east_west(u, columns_by(hx_ref, r, j))
            v = uv_ref[1, l, 8 + r : 8 + r + STRIP, :]
            north = uv_ref[1, l, 9 + r : 9 + r + STRIP, :]
            south = uv_ref[1, l, 7 + r : 7 + r + STRIP, :]
            loss = 1.0 - 2.0 * KV * wet_ref[8 + r : 8 + r + STRIP, :]
            for d, (sign, beside, own) in enumerate(
                ((-1.0, east, u), (1.0, west, u), (-1.0, north, v), (1.0, south, v))
            ):
                gate = open_ref[d, at, :]
                flow = (0.25 * sign) * (own + beside) * gate
                coef_ref[d, l, at, :] = KH * gate + flow
                loss = loss - (KH * gate - flow)
            coef_ref[4, l, at, :] = loss

    def advance(ref, t, l, r, both):
        at = slice(r, r + STRIP)
        mid = slice(8 + r, 8 + r + STRIP)
        c = ref[t, l, mid, :]
        east, west = east_west(c, both)
        fixed = isinstance(l, int)
        above = c if fixed and l == 0 else ref[t, l - 1, mid, :]
        below = c if fixed and l == levels - 1 else ref[t, l + 1, mid, :]
        return (
            coef_ref[4, l, at, :] * c
            + coef_ref[0, l, at, :] * east
            + coef_ref[1, l, at, :] * west
            + coef_ref[2, l, at, :] * ref[t, l, 9 + r : 9 + r + STRIP, :]
            + coef_ref[3, l, at, :] * ref[t, l, 7 + r : 7 + r + STRIP, :]
            + (KV * wet_ref[mid, :]) * (above + below)
        )

    def set_rows(ref, t, l, north, south):
        ref[t, l, LANES + 8 : LANES + 9, :] = north
        ref[t, l, 7:8, :] = south

    def first_step(l, carry):
        coefficients(l)
        for t in range(2):
            j = t * levels + l
            set_rows(q_ref, t, l, hn_ref[pl.ds(j, 1), :], hs_ref[pl.ds(j, 1), :])
            for r in strips:
                q1_ref[t, l, 8 + r : 8 + r + STRIP, :] = advance(
                    q_ref, t, l, r, columns_by(hx_ref, r, j)
                )
        return carry

    lax.fori_loop(1, levels - 1, first_step, 0)
    first_step(levels - 1, 0)

    own_flux.wait()
    wait_others(got_ref, a2a_recv.at[1], ROWS)
    rest_ref[...] = got_ref[:, 40:56, :].astype(F32).reshape(DEVICES * SLOTS, LANES)

    def field(f):
        body = got_ref[:, f * 8 : f * 8 + 8, :].astype(F32).reshape(DEVICES * 8, LANES)
        tails = [
            rest_ref[pl.ds(i * KEPT + f, DEVICES, stride=SLOTS), :] for i in range(TAIL)
        ]
        return jnp.concatenate([body] + tails, axis=0).astype(BF16)

    def collect(wanted):
        total = jnp.dot(
            hot_ref[...], jnp.concatenate([field(f) for f in wanted], axis=1),
            preferred_element_type=F32,
        )
        for i, f in enumerate(wanted):
            flux_ref[f] = total[:, i * LANES : (i + 1) * LANES]

    collect((3, 4))
    flux_ring = Ring(
        1, (flux_ref.at[3], hwu_ref), (flux_ref.at[3], heu_ref),
        (flux_ref.at[4, pl.ds(LANES - 8, 8)], hsv_ref), (flux_ref.at[4, pl.ds(0, 8)], hnv_ref),
    )
    flux_ring.start()
    collect((0, 1))
    collect((2,))
    wait_others(send_ref, a2a_send.at[1], ROWS)
    heat_scale = 0.3 * (1.0 - DECAY)

    def warmed(t, l, r, scale):
        at, mid = slice(r, r + STRIP), slice(8 + r, 8 + r + STRIP)
        q1_ref[t, l, mid, :] = q1_ref[t, l, mid, :] + wet_ref[mid, :] * (
            scale * flux_ref[0, at, :]
        )

    for r in strips:
        at, mid = slice(r, r + STRIP), slice(8 + r, 8 + r + STRIP)
        uv_ref[0, 0, mid, :] = uv_ref[0, 0, mid, :] + 0.1 * flux_ref[3, at, :]
        uv_ref[1, 0, mid, :] = uv_ref[1, 0, mid, :] + 0.1 * flux_ref[4, at, :]
        warmed(0, 1, r, heat_scale * DECAY)
    for t in range(2):
        j = t * levels
        set_rows(q_ref, t, 0, hn_ref[j : j + 1, :], hs_ref[j : j + 1, :])
    flux_ring.wait()
    ju = 2 * levels
    hx_ref[...] = hx_ref[...] + 0.1 * jnp.where(
        lane == 2 * ju, pltpu.roll(heu_ref[...], 2 * ju, 1),
        jnp.where(lane == 2 * ju + 1, pltpu.roll(hwu_ref[...], 2 * ju + 2, 1), 0.0),
    )
    hn_ref[ju : ju + 1, :] = hn_ref[ju : ju + 1, :] + 0.1 * hnv_ref[0:1, :]
    hs_ref[ju : ju + 1, :] = hs_ref[ju : ju + 1, :] + 0.1 * hsv_ref[7:8, :]
    coefficients(0)

    def surface(t, r):
        at = slice(r, r + STRIP)
        if t == 0:
            force = heat_scale * flux_ref[0, at, :] + 0.2 * flux_ref[1, at, :]
        else:
            force = 0.2 * flux_ref[2, at, :]
        return wet_ref[8 + r : 8 + r + STRIP, :] * force

    def surface_step(t):
        j = t * levels
        for r in strips:
            q1_ref[t, 0, 8 + r : 8 + r + STRIP, :] = advance(
                q_ref, t, 0, r, columns_by(hx_ref, r, j)
            ) + surface(t, r)

    surface_step(0)
    top_ring = Ring(
        2, (q1_ref.at[0, 0, inner], hw1_ref), (q1_ref.at[0, 0, inner], he1_ref),
        (q1_ref.at[0, 0, pl.ds(LANES, 8)], hs1_ref), (q1_ref.at[0, 0, pl.ds(8, 8)], hn1_ref),
    )
    top_ring.start()
    surface_step(1)

    def forced(l, scale):
        for r in strips:
            warmed(0, l, r, scale)
        return scale * DECAY

    lax.fori_loop(2, levels, forced, jnp.float32(heat_scale * DECAY * DECAY))

    pack_columns([strip_of(q1_ref, t, l) for t in range(2) for l in range(levels)], pe2_ref)
    for l in range(levels):
        for t in range(2):
            j = t * levels + l
            pn2_ref[j : j + 1, :] = q1_ref[t, l, LANES + 7 : LANES + 8, :]
            ps2_ref[j : j + 1, :] = q1_ref[t, l, 8:9, :]
    last_ring = Ring(
        3, (pe2_ref, hw2_ref), (pe2_ref, he2_ref), (pn2_ref, hs2_ref), (ps2_ref, hn2_ref)
    )
    last_ring.start()
    top_ring.wait()
    set_rows(q1_ref, 0, 0, hn1_ref[0:1, :], hs1_ref[7:8, :])
    for r in strips:
        q2_ref[0, 0, r : r + STRIP, :] = advance(
            q1_ref, 0, 0, r,
            jnp.where(
                slane == 0, pltpu.roll(hw1_ref[r : r + STRIP, :], 1, 1),
                pltpu.roll(he1_ref[r : r + STRIP, :], LANES - 1, 1),
            ),
        ) + surface(0, r)

    sst = q2_ref[0, 0].astype(BF16)

    def select(b, carry):
        at = pl.ds(pl.multiple_of(b * LANES, LANES), LANES)
        picked = jnp.dot(hott_ref[at, :], sst, preferred_element_type=F32).astype(BF16)
        sret_ref[pl.ds(b * 8, 8)] = picked.reshape(8, SLOTS, LANES)
        return carry

    lax.fori_loop(0, SLOTS, select, 0)
    here.each(all_to_all(2, sret_ref, ret_ref, lambda ref, i: ref.at[i, pl.ds(0, CAP)]))
    own_ret = pltpu.make_async_copy(sret_ref.at[here.me], ret_ref.at[here.me], own_sem.at[2])
    own_ret.start()

    last_ring.wait()
    join_columns(he2_ref, hw2_ref, hx2_ref)

    def second(t, l, r):
        j = t * levels + l
        return advance(q1_ref, t, l, r, columns_by(hx2_ref, r, j))

    def rows_of(t, l):
        j = t * levels + l
        set_rows(q1_ref, t, l, hn2_ref[pl.ds(j, 1), :], hs2_ref[pl.ds(j, 1), :])

    rows_of(1, 0)
    for r in strips:
        q2_ref[1, 0, r : r + STRIP, :] = second(1, 0, r) + surface(1, r)

    def second_step(l, scale):
        for t in range(2):
            rows_of(t, l)
            for r in strips:
                fresh = second(t, l, r)
                if t == 0:
                    fresh = fresh + wet_ref[8 + r : 8 + r + STRIP, :] * (
                        scale * flux_ref[0, r : r + STRIP, :]
                    )
                q2_ref[t, l, r : r + STRIP, :] = fresh
        return scale * DECAY

    scale = lax.fori_loop(1, levels - 1, second_step, jnp.float32(heat_scale * DECAY))
    second_step(levels - 1, scale)
    out_copy = pltpu.make_async_copy(q2_ref, out_hbm, out_sem)
    out_copy.start()

    own_ret.wait()
    wait_others(sret_ref, a2a_send.at[2], CAP)
    wait_others(ret_ref, a2a_recv.at[2], CAP)
    ret32_ref[pl.ds(0, DEVICES * SLOTS), :] = ret_ref[...].astype(F32).reshape(DEVICES * SLOTS, LANES)

    def backward(c, carry):
        for g in range(0, CHUNK, 8):
            base = c * CHUNK + g
            picked = jnp.concatenate(
                [ret32_ref[pl.ds(slot_ref[base + i], 1), :] for i in range(8)], axis=0
            )
            left = jnp.concatenate(
                [jnp.where(sub == i, picked, 0.0).astype(BF16) for i in range(8)], axis=1
            )
            right = w_ref[pl.ds(base, 8)].reshape(8 * LANES, LANES)
            terms_ref[pl.ds(pl.multiple_of(base, 8), 8), :] = jnp.dot(
                left, right, preferred_element_type=F32
            )
        return carry

    lax.fori_loop(0, chunks, backward, 0)
    terms = terms_ref[...]
    high = terms.astype(BF16)
    low = (terms - high.astype(F32)).astype(BF16)
    temp_ref[...] = jnp.dot(srchot_ref[...], high, preferred_element_type=F32) + jnp.dot(
        srchot_ref[...], low, preferred_element_type=F32
    )
    out_copy.wait()


def on_device(
    atm_flux, remap_weights, remap_src, remap_dst, remap_owner, tracers, currents, land_sea
):
    nonzeros, width = remap_weights.shape[0], remap_weights.shape[1]
    atm_blocks = atm_flux.shape[0]
    levels = tracers.shape[1]
    chunks = nonzeros // CHUNK

    owners = remap_owner[:, 0]
    hot = (owners[:, None] == jnp.arange(DEVICES, dtype=I32)[None, :]).astype(BF16)
    order = jnp.arange(nonzeros, dtype=I32)
    before = (order[:, None] > order[None, :]).astype(BF16)
    earlier = jnp.dot(before, hot, preferred_element_type=F32)
    position = jnp.sum(earlier * hot.astype(F32), axis=1).astype(I32)
    slot = owners * CAP + position
    taken = jnp.arange(DEVICES * CAP, dtype=I32)[:, None] == slot[None, :]
    kidx = jnp.sum(jnp.where(taken, order[None, :] - nonzeros, 0), axis=1) + nonzeros
    slot_rows = jnp.sum(jnp.where(taken, remap_dst[None, :] - 200, 0), axis=1) + 200
    row_table = jnp.pad(
        slot_rows.reshape(DEVICES, CAP).astype(F32), ((0, 0), (0, LANES - CAP)),
        constant_values=200.0,
    )

    vmem = pl.BlockSpec(memory_space=pltpu.VMEM)
    smem = pl.BlockSpec(memory_space=pltpu.SMEM)
    anywhere = pl.BlockSpec(memory_space=pl.ANY)
    padded = (2, levels, LANES + 16, LANES)
    tile = (LANES, LANES)
    scratch = [
        (remap_weights.shape, BF16), ((nonzeros + 1, 8, LANES), F32), ((8, 64, LANES), F32),
        ((DEVICES, 56, width), BF16), ((DEVICES, 56, width), BF16),
        ((DEVICES, 8, LANES), F32), ((DEVICES, 8, LANES), F32),
        ((LANES, DEVICES * CAP), BF16), ((DEVICES * SLOTS, LANES), BF16), ((DEVICES * SLOTS, LANES), F32),
        ((KEPT,) + tile, F32),
        ((DEVICES, SLOTS, width), BF16), ((DEVICES, SLOTS, width), BF16),
        ((DEVICES * SLOTS + 8, width), F32), ((nonzeros, width), F32), ((atm_blocks, nonzeros), BF16),
        (padded, F32), (padded, F32), (padded, F32), (tracers.shape, F32),
        ((5, levels) + tile, F32), ((4,) + tile, F32), ((LANES + 16, LANES), F32),
        (tile, F32), (tile, F32), (tile, F32), (tile, F32),
        (tile, F32), (tile, F32), (tile, F32), (tile, F32),
        (tile, F32), (tile, F32), ((8, LANES), F32), ((8, LANES), F32),
        (tile, F32), (tile, F32), ((8, LANES), F32), ((8, LANES), F32),
        (tile, F32), (tile, F32), (tile, F32), (tile, F32),
        (tile, F32), (tile, F32), (tile, F32), (tile, F32),
    ]
    return pl.pallas_call(
        coupled_kernel,
        name="coupled",
        out_shape=[
            jax.ShapeDtypeStruct(tracers.shape, F32),
            jax.ShapeDtypeStruct((atm_blocks, width), F32),
        ],
        in_specs=[smem, smem, smem, vmem, vmem, vmem, vmem, anywhere, anywhere, anywhere],
        out_specs=[anywhere, vmem],
        scratch_shapes=[pltpu.VMEM(shape, kind) for shape, kind in scratch]
        + [
            pltpu.SemaphoreType.DMA((chunks,)),
            pltpu.SemaphoreType.DMA((2,)),
            pltpu.SemaphoreType.DMA((3,)),
            pltpu.SemaphoreType.DMA((3,)),
            pltpu.SemaphoreType.DMA((16,)),
            pltpu.SemaphoreType.DMA((16,)),
            pltpu.SemaphoreType.DMA((3,)),
            pltpu.SemaphoreType.DMA,
        ],
        compiler_params=pltpu.CompilerParams(
            collective_id=0, has_side_effects=True, vmem_limit_bytes=64000 * 1024
        ),
    )(
        remap_src, kidx, owners * SLOTS + position, row_table, remap_src.reshape(nonzeros // LANES, LANES), atm_flux,
        land_sea, remap_weights, tracers, currents,
    )


def solution(mesh):
    tiles = P(None, None, ("sec", "gx"), "gy")
    shares = ("sec", "gx", "gy")

    def run(*args):
        return tuple(on_device(*args))

    return jax.shard_map(
        run,
        mesh=mesh,
        in_specs=(
            P(shares, None, None),
            P(shares, None, None),
            P(shares),
            P(shares),
            P(shares, None),
            tiles,
            tiles,
            P(("sec", "gx"), "gy"),
        ),
        out_specs=(tiles, P(shares, None)),
        check_vma=False,
    )
```

```python
import math

import jax
import jax.numpy as jnp
from jax import lax
from jax.experimental import pallas as pl
from jax.experimental.pallas import tpu as pltpu
from jax.sharding import PartitionSpec as P

KH = 0.1
KV = 0.1
CAP = 10
SLOTS = 16
KEPT = 5
TAIL = CAP - 8
ROWS = CAP * KEPT
LANES = 128
DEVICES = 128
CHUNK = 64
STRIP = 32
DECAY = math.exp(-0.25)
LOGICAL = pl.DeviceIdType.LOGICAL
MESH = pl.DeviceIdType.MESH
BF16 = jnp.bfloat16
F32 = jnp.float32
I32 = jnp.int32


class Torus:
    def __init__(self):
        sec, gx, gy = lax.axis_index("sec"), lax.axis_index("gx"), lax.axis_index("gy")
        self.band, self.gy = sec * 8 + gx, gy
        self.me = self.band * 8 + gy
        up, down = (self.band + 1) % 16, (self.band + 15) % 16
        self.north = (up // 8, up % 8, gy)
        self.south = (down // 8, down % 8, gy)
        self.east = (sec, gx, (gy + 1) % 8)
        self.west = (sec, gx, (gy + 7) % 8)
        self.y, self.z = (gy % 2) * 2 + sec, gx // 2
        self.xs = [((gy // 2 + d) % 4) * 2 for d in range(4)]
        self.cores = [((gx + d) % 2) * 8 for d in range(2)]

    def group(self, o):
        partners = []
        for d in (2, 1, 3, 0):
            y = (self.y + 3 - o % 4 + d) % 4
            z = (self.z + 3 - o // 4 + d) % 4
            base = (y % 2) * 64 + y // 2 + z * 16 + self.xs[d]
            partners += [base + self.cores[c] for c in (1, 0)]
        return partners

    def send_group(self, o, act):
        partners = self.group(o)
        for p in partners[:-1]:
            act(p)

        @pl.when(o < 15)
        def _():
            act(partners[-1])

    def each(self, act):
        def body(o, carry):
            self.send_group(o, act)
            return carry

        lax.fori_loop(0, 16, body, 0)


def wait_others(ref, sem, rows):
    first = pl.ds(0, DEVICES - 1)
    view = ref.at[first, pl.ds(0, rows)]
    pltpu.make_async_copy(view, view, sem).wait()


def coupled_kernel(
    src_ref, kidx_ref, slot_ref, row_ref, srcrow_ref, atm_ref, land_ref, w_hbm, q_hbm, uv_hbm,
    out_hbm, temp_ref,
    w_ref, part_ref, tmp_ref, send_ref, got_ref, srow_ref, rrow_ref, hot_ref, hott_ref, rest_ref,
    flux_ref, sret_ref, ret_ref, ret32_ref, terms_ref, srchot_ref,
    q_ref, uv_ref, q1_ref, q2_ref, coef_ref, open_ref, wet_ref,
    pe_ref, hx_ref, he_ref, hw_ref, pn_ref, ps_ref, hn_ref, hs_ref,
    heu_ref, hwu_ref, hnv_ref, hsv_ref,
    he1_ref, hw1_ref, hn1_ref, hs1_ref,
    pe2_ref, hx2_ref, he2_ref, hw2_ref, pn2_ref, ps2_ref, hn2_ref, hs2_ref,
    w_sem, in_sem, a2a_send, a2a_recv, side_send, side_recv, own_sem, out_sem,
):
    here = Torus()
    nonzeros = w_ref.shape[0]
    chunks = nonzeros // CHUNK
    levels = q_ref.shape[1]
    inner = pl.ds(8, LANES)

    def weight_copy(c):
        part = pl.ds(c * CHUNK, CHUNK)
        return pltpu.make_async_copy(w_hbm.at[part], w_ref.at[part], w_sem.at[c])

    def start_weights(c, carry):
        weight_copy(c).start()
        return carry

    q_copy = pltpu.make_async_copy(q_hbm, q_ref.at[:, :, inner], in_sem.at[0])
    uv_copy = pltpu.make_async_copy(uv_hbm, uv_ref.at[:, :, inner], in_sem.at[1])
    q_copy.start()
    uv_copy.start()
    lax.fori_loop(0, chunks, start_weights, 0)

    got_ref[...] = jnp.zeros_like(got_ref)
    barrier = pltpu.get_barrier_semaphore()
    here.each(
        lambda p: pl.semaphore_signal(barrier, inc=1, device_id=p, device_id_type=LOGICAL)
    )
    srow_ref[:, 0:1, :] = row_ref[...].reshape(DEVICES, 1, LANES)
    part_ref[nonzeros] = jnp.zeros((8, LANES), F32)
    pn_ref[...] = jnp.zeros_like(pn_ref)
    ps_ref[...] = jnp.zeros_like(ps_ref)
    pn2_ref[...] = jnp.zeros_like(pn2_ref)
    ps2_ref[...] = jnp.zeros_like(ps2_ref)

    sub = lax.broadcasted_iota(I32, (8, LANES), 0)
    takes = [
        jnp.where(sub < 2, 1.0, 0.0),
        jnp.where(sub == 1, 1.0, 0.0),
        jnp.where((sub == 1) | (sub == 2), 1.0, 0.0),
        jnp.where(sub == 2, -0.5, jnp.where((sub == 3) | (sub == 4), 1.0, 0.0)),
        jnp.where(sub == 1, -0.75, 0.0),
    ]
    blank = jnp.zeros((8, LANES), BF16)

    def combine(p):
        p = p.astype(BF16).astype(F32)
        total = p * takes[0]
        for up in range(1, 5):
            total = total + pltpu.roll(p, 8 - up, 0) * takes[up]
        return total

    def forward(c, carry):
        weight_copy(c).wait()
        for i in range(0, CHUNK, 2):
            k = c * CHUNK + i
            left = jnp.concatenate(
                [
                    jnp.concatenate([atm_ref[src_ref[k]], blank], axis=1),
                    jnp.concatenate([blank, atm_ref[src_ref[k + 1]]], axis=1),
                ],
                axis=0,
            )
            right = jnp.concatenate([w_ref[k], w_ref[k + 1]], axis=1)
            p = lax.dot_general(
                left, right, (((1,), (1,)), ((), ())), preferred_element_type=F32
            )
            part_ref[k] = combine(p[:8])
            part_ref[k + 1] = combine(p[8:])
        return carry

    def all_to_all(index, src, dst, cut):
        def act(p):
            pltpu.make_async_remote_copy(
                cut(src, p), cut(dst, here.me), a2a_send.at[index], a2a_recv.at[index],
                device_id=p, device_id_type=LOGICAL,
            ).start()

        return act

    class Ring:
        def __init__(self, index, east, west, north, south):
            self.index, self.pairs = index, (east, west, north, south)

        def start(self):
            targets = (here.east, here.west, here.north, here.south)
            for d, ((src, dst), target) in enumerate(zip(self.pairs, targets)):
                whole = pl.ds(0, src.shape[0])
                pltpu.make_async_remote_copy(
                    src.at[whole], dst.at[whole], side_send.at[self.index * 4 + d],
                    side_recv.at[self.index * 4 + d], device_id=target, device_id_type=MESH,
                ).start()

        def wait(self):
            for d, (src, dst) in enumerate(self.pairs):
                whole = pl.ds(0, src.shape[0])
                at = self.index * 4 + d
                pltpu.make_async_copy(src.at[whole], src.at[whole], side_send.at[at]).wait()
                pltpu.make_async_copy(dst.at[whole], dst.at[whole], side_recv.at[at]).wait()

    lane = lax.broadcasted_iota(I32, (LANES, LANES), 1)

    slane = lax.broadcasted_iota(I32, (STRIP, LANES), 1)
    pair = slane // 2
    strips = range(0, LANES, STRIP)

    def pack_columns(tiles, out_ref):
        for r in strips:
            packed = jnp.zeros((STRIP, LANES), F32)
            for i, tile in enumerate(tiles):
                packed = jnp.where(pair == i, pltpu.roll(tile(r), 2 * i + 1, 1), packed)
            out_ref[r : r + STRIP, :] = packed

    def join_columns(east_ref, west_ref, out_ref):
        for r in strips:
            at = slice(r, r + STRIP)
            out_ref[at, :] = jnp.where(
                slane % 2 == 0, pltpu.roll(east_ref[at, :], LANES - 1, 1),
                pltpu.roll(west_ref[at, :], 1, 1),
            )

    def strip_of(ref, *lead):
        return lambda r: ref[(*lead, slice(8 + r, 8 + r + STRIP), slice(None))]

    wet_ref[...] = jnp.zeros_like(wet_ref)
    wet_ref[inner, :] = land_ref[...].astype(F32)
    q_copy.wait()
    uv_copy.wait()

    jw = 3 * levels
    pack_columns(
        [strip_of(q_ref, t, l) for t in range(2) for l in range(levels)]
        + [strip_of(uv_ref, 0, l) for l in range(levels)]
        + [strip_of(wet_ref)],
        pe_ref,
    )
    for l in range(levels):
        for t in range(2):
            j = t * levels + l
            pn_ref[j : j + 1, :] = q_ref[t, l, LANES + 7 : LANES + 8, :]
            ps_ref[j : j + 1, :] = q_ref[t, l, 8:9, :]
        j = 2 * levels + l
        pn_ref[j : j + 1, :] = uv_ref[1, l, LANES + 7 : LANES + 8, :]
        ps_ref[j : j + 1, :] = uv_ref[1, l, 8:9, :]
    pn_ref[jw : jw + 1, :] = wet_ref[LANES + 7 : LANES + 8, :]
    ps_ref[jw : jw + 1, :] = wet_ref[8:9, :]
    inputs_ring = Ring(
        0, (pe_ref, hw_ref), (pe_ref, he_ref), (pn_ref, hs_ref), (ps_ref, hn_ref)
    )

    lax.fori_loop(0, chunks // 2, forward, 0)
    pl.semaphore_wait(barrier, DEVICES - 1)
    here.each(all_to_all(0, srow_ref, rrow_ref, lambda ref, i: ref.at[i, pl.ds(0, 1)]))
    inputs_ring.start()
    lax.fori_loop(chunks // 2, chunks, forward, 0)
    send_flux = all_to_all(1, send_ref, got_ref, lambda ref, i: ref.at[i, pl.ds(0, ROWS)])

    def pack(o, carry):
        partners = here.group(o)
        for i, p in enumerate(partners):
            found = [part_ref[kidx_ref[p * CAP + s]] for s in range(CAP)]
            for s in range(8):
                tmp_ref[i, s * 8 : s * 8 + 8, :] = found[s]
            shifted = pltpu.roll(found[9], KEPT, 0)
            send_ref[p, 40:48] = jnp.where(sub < KEPT, found[8], shifted).astype(BF16)
            send_ref[p, 48:56] = shifted.astype(BF16)
        for i, p in enumerate(partners):
            for f in range(KEPT):
                send_ref[p, f * 8 : f * 8 + 8] = tmp_ref[
                    i, pl.ds(f, 8, stride=8), :
                ].astype(BF16)

        @pl.when(o > 0)
        def _():
            here.send_group(o - 1, send_flux)

        return carry

    lax.fori_loop(0, 16, pack, 0)
    own_rows = pltpu.make_async_copy(
        srow_ref.at[here.me, pl.ds(0, 1)], rrow_ref.at[here.me, pl.ds(0, 1)], own_sem.at[0]
    )
    own_rows.start()
    here.send_group(15, send_flux)
    own_flux = pltpu.make_async_copy(send_ref.at[here.me], got_ref.at[here.me], own_sem.at[1])
    own_flux.start()

    own_rows.wait()
    wait_others(srow_ref, a2a_send.at[0], 1)
    wait_others(rrow_ref, a2a_recv.at[0], 1)
    rows = rrow_ref[:, 0:1, :].reshape(DEVICES, LANES).astype(BF16)
    upright = lax.broadcasted_iota(I32, (LANES, LANES), 0)
    ones = jnp.ones((LANES, LANES), BF16)

    def spread_rows(b, each):
        pick = (lane == b * (LANES // each) + upright // each).astype(F32).astype(BF16)
        spread = jnp.dot(pick, rows, preferred_element_type=F32)
        return jnp.where(lane == upright % each, spread, 0.0).astype(BF16)

    for b in range(SLOTS):
        down = jnp.dot(spread_rows(b, SLOTS), ones, preferred_element_type=F32)
        hott_ref[b * LANES : (b + 1) * LANES, :] = (
            (down == lane.astype(F32)).astype(F32).astype(BF16)
        )
    for b in range(8):
        across = lax.dot_general(
            ones, spread_rows(b, 8), (((1,), (1,)), ((), ())), preferred_element_type=F32
        )
        hot_ref[:, b * LANES : (b + 1) * LANES] = (
            (across == upright.astype(F32)).astype(F32).astype(BF16)
        )
    turned = jnp.transpose(rrow_ref[:, 0:1, :].reshape(DEVICES, LANES))
    for i in range(TAIL):
        hot_ref[:, (8 + i) * LANES : (9 + i) * LANES] = (
            (turned[8 + i : 9 + i, :] == upright.astype(F32)).astype(F32).astype(BF16)
        )
    blocks = temp_ref.shape[0]
    block = lax.broadcasted_iota(I32, (blocks, LANES), 0)
    for i in range(nonzeros // LANES):
        srchot_ref[:, i * LANES : (i + 1) * LANES] = (
            (block == srcrow_ref[i : i + 1, :]).astype(F32).astype(BF16)
        )

    inputs_ring.wait()
    inside_e = jnp.where(here.gy < 7, 1.0, 0.0)
    inside_w = jnp.where(here.gy > 0, 1.0, 0.0)
    inside_n = jnp.where(here.band < 15, 1.0, 0.0)
    inside_s = jnp.where(here.band > 0, 1.0, 0.0)
    wet_ref[LANES + 8 : LANES + 9, :] = hn_ref[jw : jw + 1, :] * inside_n
    wet_ref[7:8, :] = hs_ref[jw : jw + 1, :] * inside_s
    join_columns(he_ref, hw_ref, hx_ref)

    def columns_by(ref, r, i):
        return pltpu.roll(ref[r : r + STRIP, :], LANES - 1 - 2 * i, 1)

    def east_west(tile, both):
        return (
            jnp.where(slane == LANES - 1, both, pltpu.roll(tile, LANES - 1, 1)),
            jnp.where(slane == 0, both, pltpu.roll(tile, 1, 1)),
        )

    for r in strips:
        wet = wet_ref[8 + r : 8 + r + STRIP, :]
        both = columns_by(hx_ref, r, jw)
        east, west = east_west(wet, jnp.where(slane == 0, both * inside_w, both * inside_e))
        open_ref[0, r : r + STRIP, :] = wet * east
        open_ref[1, r : r + STRIP, :] = wet * west
        open_ref[2, r : r + STRIP, :] = wet * wet_ref[9 + r : 9 + r + STRIP, :]
        open_ref[3, r : r + STRIP, :] = wet * wet_ref[7 + r : 7 + r + STRIP, :]

    def coefficients(l):
        j = 2 * levels + l
        uv_ref[1, l, LANES + 8 : LANES + 9, :] = hn_ref[pl.ds(j, 1), :]
        uv_ref[1, l, 7:8, :] = hs_ref[pl.ds(j, 1), :]
        for r in strips:
            at = slice(r, r + STRIP)
            u = uv_ref[0, l, 8 + r : 8 + r + STRIP, :]
            east, west = east_west(u, columns_by(hx_ref, r, j))
            v = uv_ref[1, l, 8 + r : 8 + r + STRIP, :]
            north = uv_ref[1, l, 9 + r : 9 + r + STRIP, :]
            south = uv_ref[1, l, 7 + r : 7 + r + STRIP, :]
            loss = 1.0 - 2.0 * KV * wet_ref[8 + r : 8 + r + STRIP, :]
            for d, (sign, beside, own) in enumerate(
                ((-1.0, east, u), (1.0, west, u), (-1.0, north, v), (1.0, south, v))
            ):
                gate = open_ref[d, at, :]
                flow = (0.25 * sign) * (own + beside) * gate
                coef_ref[d, l, at, :] = KH * gate + flow
                loss = loss - (KH * gate - flow)
            coef_ref[4, l, at, :] = loss

    def advance(ref, t, l, r, both):
        at = slice(r, r + STRIP)
        mid = slice(8 + r, 8 + r + STRIP)
        c = ref[t, l, mid, :]
        east, west = east_west(c, both)
        fixed = isinstance(l, int)
        above = c if fixed and l == 0 else ref[t, l - 1, mid, :]
        below = c if fixed and l == levels - 1 else ref[t, l + 1, mid, :]
        return (
            coef_ref[4, l, at, :] * c
            + coef_ref[0, l, at, :] * east
            + coef_ref[1, l, at, :] * west
            + coef_ref[2, l, at, :] * ref[t, l, 9 + r : 9 + r + STRIP, :]
            + coef_ref[3, l, at, :] * ref[t, l, 7 + r : 7 + r + STRIP, :]
            + (KV * wet_ref[mid, :]) * (above + below)
        )

    def set_rows(ref, t, l, north, south):
        ref[t, l, LANES + 8 : LANES + 9, :] = north
        ref[t, l, 7:8, :] = south

    def first_step(l, carry):
        coefficients(l)
        for t in range(2):
            j = t * levels + l
            set_rows(q_ref, t, l, hn_ref[pl.ds(j, 1), :], hs_ref[pl.ds(j, 1), :])
            for r in strips:
                q1_ref[t, l, 8 + r : 8 + r + STRIP, :] = advance(
                    q_ref, t, l, r, columns_by(hx_ref, r, j)
                )
        return carry

    lax.fori_loop(1, levels - 1, first_step, 0)
    first_step(levels - 1, 0)

    own_flux.wait()
    wait_others(got_ref, a2a_recv.at[1], ROWS)
    rest_ref[...] = got_ref[:, 40:56, :].astype(F32).reshape(DEVICES * SLOTS, LANES)

    def field(f):
        body = got_ref[:, f * 8 : f * 8 + 8, :].astype(F32).reshape(DEVICES * 8, LANES)
        tails = [
            rest_ref[pl.ds(i * KEPT + f, DEVICES, stride=SLOTS), :] for i in range(TAIL)
        ]
        return jnp.concatenate([body] + tails, axis=0).astype(BF16)

    def collect(wanted):
        total = jnp.dot(
            hot_ref[...], jnp.concatenate([field(f) for f in wanted], axis=1),
            preferred_element_type=F32,
        )
        for i, f in enumerate(wanted):
            flux_ref[f] = total[:, i * LANES : (i + 1) * LANES]

    collect((3, 4))
    flux_ring = Ring(
        1, (flux_ref.at[3], hwu_ref), (flux_ref.at[3], heu_ref),
        (flux_ref.at[4, pl.ds(LANES - 8, 8)], hsv_ref), (flux_ref.at[4, pl.ds(0, 8)], hnv_ref),
    )
    flux_ring.start()
    collect((0, 1))
    collect((2,))
    wait_others(send_ref, a2a_send.at[1], ROWS)
    heat_scale = 0.3 * (1.0 - DECAY)

    def warmed(t, l, r, scale):
        at, mid = slice(r, r + STRIP), slice(8 + r, 8 + r + STRIP)
        q1_ref[t, l, mid, :] = q1_ref[t, l, mid, :] + wet_ref[mid, :] * (
            scale * flux_ref[0, at, :]
        )

    for r in strips:
        at, mid = slice(r, r + STRIP), slice(8 + r, 8 + r + STRIP)
        uv_ref[0, 0, mid, :] = uv_ref[0, 0, mid, :] + 0.1 * flux_ref[3, at, :]
        uv_ref[1, 0, mid, :] = uv_ref[1, 0, mid, :] + 0.1 * flux_ref[4, at, :]
        warmed(0, 1, r, heat_scale * DECAY)
    for t in range(2):
        j = t * levels
        set_rows(q_ref, t, 0, hn_ref[j : j + 1, :], hs_ref[j : j + 1, :])
    flux_ring.wait()
    ju = 2 * levels
    hx_ref[...] = hx_ref[...] + 0.1 * jnp.where(
        lane == 2 * ju, pltpu.roll(heu_ref[...], 2 * ju, 1),
        jnp.where(lane == 2 * ju + 1, pltpu.roll(hwu_ref[...], 2 * ju + 2, 1), 0.0),
    )
    hn_ref[ju : ju + 1, :] = hn_ref[ju : ju + 1, :] + 0.1 * hnv_ref[0:1, :]
    hs_ref[ju : ju + 1, :] = hs_ref[ju : ju + 1, :] + 0.1 * hsv_ref[7:8, :]
    coefficients(0)

    def surface(t, r):
        at = slice(r, r + STRIP)
        if t == 0:
            force = heat_scale * flux_ref[0, at, :] + 0.2 * flux_ref[1, at, :]
        else:
            force = 0.2 * flux_ref[2, at, :]
        return wet_ref[8 + r : 8 + r + STRIP, :] * force

    def surface_step(t):
        j = t * levels
        for r in strips:
            q1_ref[t, 0, 8 + r : 8 + r + STRIP, :] = advance(
                q_ref, t, 0, r, columns_by(hx_ref, r, j)
            ) + surface(t, r)

    surface_step(0)
    top_ring = Ring(
        2, (q1_ref.at[0, 0, inner], hw1_ref), (q1_ref.at[0, 0, inner], he1_ref),
        (q1_ref.at[0, 0, pl.ds(LANES, 8)], hs1_ref), (q1_ref.at[0, 0, pl.ds(8, 8)], hn1_ref),
    )
    top_ring.start()
    surface_step(1)

    def forced(l, scale):
        for r in strips:
            warmed(0, l, r, scale)
        return scale * DECAY

    lax.fori_loop(2, levels, forced, jnp.float32(heat_scale * DECAY * DECAY))

    pack_columns([strip_of(q1_ref, t, l) for t in range(2) for l in range(levels)], pe2_ref)
    for l in range(levels):
        for t in range(2):
            j = t * levels + l
            pn2_ref[j : j + 1, :] = q1_ref[t, l, LANES + 7 : LANES + 8, :]
            ps2_ref[j : j + 1, :] = q1_ref[t, l, 8:9, :]
    last_ring = Ring(
        3, (pe2_ref, hw2_ref), (pe2_ref, he2_ref), (pn2_ref, hs2_ref), (ps2_ref, hn2_ref)
    )
    last_ring.start()
    top_ring.wait()
    set_rows(q1_ref, 0, 0, hn1_ref[0:1, :], hs1_ref[7:8, :])
    for r in strips:
        q2_ref[0, 0, r : r + STRIP, :] = advance(
            q1_ref, 0, 0, r,
            jnp.where(
                slane == 0, pltpu.roll(hw1_ref[r : r + STRIP, :], 1, 1),
                pltpu.roll(he1_ref[r : r + STRIP, :], LANES - 1, 1),
            ),
        ) + surface(0, r)

    sst = q2_ref[0, 0].astype(BF16)

    def select(b, carry):
        at = pl.ds(pl.multiple_of(b * LANES, LANES), LANES)
        picked = jnp.dot(hott_ref[at, :], sst, preferred_element_type=F32).astype(BF16)
        sret_ref[pl.ds(b * 8, 8)] = picked.reshape(8, SLOTS, LANES)
        return carry

    lax.fori_loop(0, SLOTS, select, 0)
    here.each(all_to_all(2, sret_ref, ret_ref, lambda ref, i: ref.at[i, pl.ds(0, CAP)]))
    own_ret = pltpu.make_async_copy(sret_ref.at[here.me], ret_ref.at[here.me], own_sem.at[2])
    own_ret.start()

    last_ring.wait()
    join_columns(he2_ref, hw2_ref, hx2_ref)

    def second(t, l, r):
        j = t * levels + l
        return advance(q1_ref, t, l, r, columns_by(hx2_ref, r, j))

    def rows_of(t, l):
        j = t * levels + l
        set_rows(q1_ref, t, l, hn2_ref[pl.ds(j, 1), :], hs2_ref[pl.ds(j, 1), :])

    rows_of(1, 0)
    for r in strips:
        q2_ref[1, 0, r : r + STRIP, :] = second(1, 0, r) + surface(1, r)

    def second_step(l, scale):
        for t in range(2):
            rows_of(t, l)
            for r in strips:
                fresh = second(t, l, r)
                if t == 0:
                    fresh = fresh + wet_ref[8 + r : 8 + r + STRIP, :] * (
                        scale * flux_ref[0, r : r + STRIP, :]
                    )
                q2_ref[t, l, r : r + STRIP, :] = fresh
        return scale * DECAY

    scale = lax.fori_loop(1, levels - 1, second_step, jnp.float32(heat_scale * DECAY))
    second_step(levels - 1, scale)
    out_copy = pltpu.make_async_copy(q2_ref, out_hbm, out_sem)
    out_copy.start()

    own_ret.wait()
    wait_others(sret_ref, a2a_send.at[2], CAP)
    wait_others(ret_ref, a2a_recv.at[2], CAP)
    ret32_ref[pl.ds(0, DEVICES * SLOTS), :] = ret_ref[...].astype(F32).reshape(DEVICES * SLOTS, LANES)

    def backward(c, carry):
        for g in range(0, CHUNK, 8):
            base = c * CHUNK + g
            picked = jnp.concatenate(
                [ret32_ref[pl.ds(slot_ref[base + i], 1), :] for i in range(8)], axis=0
            )
            left = jnp.concatenate(
                [jnp.where(sub == i, picked, 0.0).astype(BF16) for i in range(8)], axis=1
            )
            right = w_ref[pl.ds(base, 8)].reshape(8 * LANES, LANES)
            terms_ref[pl.ds(pl.multiple_of(base, 8), 8), :] = jnp.dot(
                left, right, preferred_element_type=F32
            )
        return carry

    lax.fori_loop(0, chunks, backward, 0)
    terms = terms_ref[...]
    high = terms.astype(BF16)
    low = (terms - high.astype(F32)).astype(BF16)
    temp_ref[...] = jnp.dot(srchot_ref[...], high, preferred_element_type=F32) + jnp.dot(
        srchot_ref[...], low, preferred_element_type=F32
    )
    out_copy.wait()


def on_device(
    atm_flux, remap_weights, remap_src, remap_dst, remap_owner, tracers, currents, land_sea
):
    nonzeros, width = remap_weights.shape[0], remap_weights.shape[1]
    atm_blocks = atm_flux.shape[0]
    levels = tracers.shape[1]
    chunks = nonzeros // CHUNK

    owners = remap_owner[:, 0]
    hot = (owners[:, None] == jnp.arange(DEVICES, dtype=I32)[None, :]).astype(BF16)
    order = jnp.arange(nonzeros, dtype=I32)
    before = (order[:, None] > order[None, :]).astype(BF16)
    earlier = jnp.dot(before, hot, preferred_element_type=F32)
    position = jnp.sum(earlier * hot.astype(F32), axis=1).astype(I32)
    slot = owners * CAP + position
    taken = jnp.arange(DEVICES * CAP, dtype=I32)[:, None] == slot[None, :]
    kidx = jnp.sum(jnp.where(taken, order[None, :] - nonzeros, 0), axis=1) + nonzeros
    slot_rows = jnp.sum(jnp.where(taken, remap_dst[None, :] - 200, 0), axis=1) + 200
    row_table = jnp.pad(
        slot_rows.reshape(DEVICES, CAP).astype(F32), ((0, 0), (0, LANES - CAP)),
        constant_values=200.0,
    )

    vmem = pl.BlockSpec(memory_space=pltpu.VMEM)
    smem = pl.BlockSpec(memory_space=pltpu.SMEM)
    anywhere = pl.BlockSpec(memory_space=pl.ANY)
    padded = (2, levels, LANES + 16, LANES)
    tile = (LANES, LANES)
    scratch = [
        (remap_weights.shape, BF16), ((nonzeros + 1, 8, LANES), F32), ((8, 64, LANES), F32),
        ((DEVICES, 56, width), BF16), ((DEVICES, 56, width), BF16),
        ((DEVICES, 8, LANES), F32), ((DEVICES, 8, LANES), F32),
        ((LANES, DEVICES * CAP), BF16), ((DEVICES * SLOTS, LANES), BF16), ((DEVICES * SLOTS, LANES), F32),
        ((KEPT,) + tile, F32),
        ((DEVICES, SLOTS, width), BF16), ((DEVICES, SLOTS, width), BF16),
        ((DEVICES * SLOTS + 8, width), F32), ((nonzeros, width), F32), ((atm_blocks, nonzeros), BF16),
        (padded, F32), (padded, F32), (padded, F32), (tracers.shape, F32),
        ((5, levels) + tile, F32), ((4,) + tile, F32), ((LANES + 16, LANES), F32),
        (tile, F32), (tile, F32), (tile, F32), (tile, F32),
        (tile, F32), (tile, F32), (tile, F32), (tile, F32),
        (tile, F32), (tile, F32), ((8, LANES), F32), ((8, LANES), F32),
        (tile, F32), (tile, F32), ((8, LANES), F32), ((8, LANES), F32),
        (tile, F32), (tile, F32), (tile, F32), (tile, F32),
        (tile, F32), (tile, F32), (tile, F32), (tile, F32),
    ]
    return pl.pallas_call(
        coupled_kernel,
        name="coupled",
        out_shape=[
            jax.ShapeDtypeStruct(tracers.shape, F32),
            jax.ShapeDtypeStruct((atm_blocks, width), F32),
        ],
        in_specs=[smem, smem, smem, vmem, vmem, vmem, vmem, anywhere, anywhere, anywhere],
        out_specs=[anywhere, vmem],
        scratch_shapes=[pltpu.VMEM(shape, kind) for shape, kind in scratch]
        + [
            pltpu.SemaphoreType.DMA((chunks,)),
            pltpu.SemaphoreType.DMA((2,)),
            pltpu.SemaphoreType.DMA((3,)),
            pltpu.SemaphoreType.DMA((3,)),
            pltpu.SemaphoreType.DMA((16,)),
            pltpu.SemaphoreType.DMA((16,)),
            pltpu.SemaphoreType.DMA((3,)),
            pltpu.SemaphoreType.DMA,
        ],
        compiler_params=pltpu.CompilerParams(
            collective_id=0, has_side_effects=True, vmem_limit_bytes=64000 * 1024
        ),
    )(
        remap_src, kidx, owners * SLOTS + position, row_table, remap_src.reshape(nonzeros // LANES, LANES), atm_flux,
        land_sea, remap_weights, tracers, currents,
    )


def solution(mesh):
    tiles = P(None, None, ("sec", "gx"), "gy")
    shares = ("sec", "gx", "gy")

    def run(*args):
        return tuple(on_device(*args))

    return jax.shard_map(
        run,
        mesh=mesh,
        in_specs=(
            P(shares, None, None),
            P(shares, None, None),
            P(shares),
            P(shares),
            P(shares, None),
            tiles,
            tiles,
            P(("sec", "gx"), "gy"),
        ),
        out_specs=(tiles, P(shares, None)),
        check_vma=False,
    )
```
